32 devices in a mesh: chan: 8 (over y, x, core), win: 4 (over z).
Axes of the slice: x: 2, y: 2, z: 4, core: 2. Of those that a mesh axis runs over, the one named last changes fastest.
Arguments:
- records: float32 [16, 1024, 256], P('win', 'chan'), may hold values from -180 to 180
- sources: int32 [32], replicated, may hold values from 0 to 255, as said below
Outputs:
- correlations: float32 [32, 256, 256], P('win', None, 'chan')
The draws below stay inside these ranges and needn't reach their ends.
Inputs may be any that keep to these rules, and one draw needn't show every extreme that they name: `sources`: source s is one of the channels s * 8 to (s + 1) * 8 - 1; the first source is channel 0 and the last is channel 256 - 1.
All inputs are finite; a program needn't handle non-finite values.
Results may differ from the reference program's by a relative error of at most 0.00022.
Values sent between devices are 32-bit elements; how exact they have to be, the bound alone decides.
A program may use at most 64 MiB of HBM per device.

```python
import math
import jax
import jax.numpy as jnp
from jax import lax

L = 1024
W = 16
C = 256
NS = 32
LAGS = 256
HALF = 16
REACH = 32


def draw_records(key, part):
    subkeys = jax.random.split(key, 3)
    channel_gain = jnp.exp(jax.random.uniform(subkeys[0], (1, 1, C), minval=math.log(0.1), maxval=math.log(10.0)))
    segments = L // 16
    envelope = jnp.exp(jax.random.uniform(subkeys[1], (W, 16, C), minval=math.log(0.3), maxval=math.log(3.0)))
    envelope = jnp.repeat(envelope, segments, axis=1)
    random_part = jax.random.truncated_normal(subkeys[2], -6.0, 6.0, (W, L, C))
    return (channel_gain * envelope * random_part).astype(jnp.float32)


def draw_sources(key, part):
    spacing = C // NS
    offsets = jax.random.randint(key, (NS,), 0, spacing).astype(jnp.int32)
    offsets = offsets.at[0].set(0).at[NS - 1].set(spacing - 1)
    return (jnp.arange(NS, dtype=jnp.int32) * spacing + offsets).astype(jnp.int32)


def setup_inputs(seed: int = 0) -> dict:
    arg_keys = jax.random.split(jax.random.key(seed), 3)
    records = draw_records(jax.random.fold_in(arg_keys[2], 71), 0)
    sources = draw_sources(jax.random.fold_in(arg_keys[2], 71), 0)
    return {"records": records, "sources": sources}


HIGHEST = lax.Precision.HIGHEST
AMPLITUDE_FLOOR = 0.25
WHITE_EPSILON = 1e-06

def fourier_table(length):
    freq_count = length // 2
    freqs = jnp.arange(freq_count, dtype=jnp.int32)[:, None]
    sample_index = jnp.arange(length, dtype=jnp.int32)[None, :]
    angles = (freqs * sample_index % length).astype(jnp.float32) * (2.0 * math.pi / length)
    return jnp.concatenate([jnp.cos(angles), -jnp.sin(angles)], axis=0)

def band_table(freq_count, reach):
    rows_index = jnp.arange(freq_count, dtype=jnp.int32)[:, None]
    cols_index = jnp.arange(freq_count, dtype=jnp.int32)[None, :]
    return (jnp.abs(rows_index - cols_index) <= reach).astype(jnp.float32)

def inverse_table(length, lag_count, first_bin, bin_count, factor):
    freqs = first_bin + jnp.arange(bin_count, dtype=jnp.int32)
    lag_index = jnp.arange(lag_count, dtype=jnp.int32) - lag_count // 2
    angles = (lag_index[:, None] * freqs[None, :] % length).astype(jnp.float32) * (2.0 * math.pi / length)
    weights = jnp.where(freqs == 0, 1.0, 2.0).astype(jnp.float32)[None, :] * factor
    return jnp.concatenate([weights * jnp.cos(angles), -weights * jnp.sin(angles)], axis=1)

def reference(records, sources):
    freq_count = L // 2
    forward = fourier_table(L)
    band_matrix = band_table(freq_count, REACH)
    window_span = 2 * HALF + 1

    def one_window(window_data):
        chans = window_data.shape[1]
        padded = jnp.pad(jnp.abs(window_data), ((HALF, HALF), (0, 0)))
        running = jnp.concatenate([jnp.zeros((1, chans), jnp.float32), jnp.cumsum(padded, axis=0)], axis=0)
        amplitude = (running[window_span:] - running[:L]) / window_span
        normalized = window_data / jnp.maximum(amplitude, AMPLITUDE_FLOOR)
        spectrum = jnp.dot(forward, normalized, precision=HIGHEST)
        real_part = spectrum[:freq_count]
        imag_part = spectrum[freq_count:]
        magnitude = jnp.sqrt(real_part * real_part + imag_part * imag_part)
        smoothed = jnp.dot(band_matrix, magnitude, precision=HIGHEST) / (2 * REACH + 1) + WHITE_EPSILON
        return jnp.stack([real_part / smoothed, imag_part / smoothed])
    source_white = lax.map(one_window, records[:, :, sources])

    def accumulate(carry, pair):
        window_data, source_part = pair
        whitened = one_window(window_data)
        source_real = source_part[0][:, :, None]
        source_imag = source_part[1][:, :, None]
        white_real = whitened[0][:, None, :]
        white_imag = whitened[1][:, None, :]
        cross_real = carry[0] + source_real * white_real + source_imag * white_imag
        cross_imag = carry[1] + source_real * white_imag - source_imag * white_real
        return ((cross_real, cross_imag), None)
    chans = records.shape[2]
    zeros_init = jnp.zeros((freq_count, NS, chans), jnp.float32)
    (cross_real, cross_imag), _ = lax.scan(accumulate, (zeros_init, zeros_init), (records, source_white))
    factor = 1.0 / math.sqrt(W * freq_count)
    table = inverse_table(L, LAGS, 0, freq_count, factor).reshape(LAGS, 2, freq_count)
    stacked = jnp.stack([cross_real, cross_imag])
    return jnp.einsum('tak,aksc->stc', table, stacked, precision=HIGHEST)
```

```python
import functools
import math

import jax
import jax.numpy as jnp
import numpy as np
from jax import lax
from jax.experimental import pallas as pl
from jax.experimental.pallas import tpu as pltpu
from jax.sharding import PartitionSpec as P

HIGHEST = lax.Precision.HIGHEST
AMPLITUDE_FLOOR = 0.25
WHITE_EPSILON = 1e-06


def fourier_table(length):
    freq_count = length // 2
    freqs = jnp.arange(freq_count, dtype=jnp.int32)[:, None]
    sample_index = jnp.arange(length, dtype=jnp.int32)[None, :]
    angles = (freqs * sample_index % length).astype(jnp.float32) * (2.0 * math.pi / length)
    return jnp.concatenate([jnp.cos(angles), -jnp.sin(angles)], axis=0)


def band_table(freq_count, reach):
    rows_index = jnp.arange(freq_count, dtype=jnp.int32)[:, None]
    cols_index = jnp.arange(freq_count, dtype=jnp.int32)[None, :]
    return (jnp.abs(rows_index - cols_index) <= reach).astype(jnp.float32)


def inverse_table(length, lag_count, first_bin, bin_count, factor):
    freqs = first_bin + jnp.arange(bin_count, dtype=jnp.int32)
    lag_index = jnp.arange(lag_count, dtype=jnp.int32) - lag_count // 2
    angles = (lag_index[:, None] * freqs[None, :] % length).astype(jnp.float32) * (
        2.0 * math.pi / length
    )
    weights = jnp.where(freqs == 0, 1.0, 2.0).astype(jnp.float32)[None, :] * factor
    return jnp.concatenate([weights * jnp.cos(angles), -weights * jnp.sin(angles)], axis=1)


def running_level(padded, time_count, window_span):
    window_total = padded.shape[0]
    chans = padded.shape[2]
    running = jnp.concatenate(
        [jnp.zeros((window_total, 1, chans), jnp.float32), jnp.cumsum(jnp.abs(padded), axis=1)],
        axis=1,
    )
    return (running[:, window_span:] - running[:, :time_count]) / window_span


def local(records, sources):
    chan_count = lax.axis_size("chan")
    local_windows, local_time, all_channels = records.shape
    length = local_time * chan_count
    freq_count = length // 2
    chan_width = all_channels // chan_count
    half_width = min(16, local_time)
    smooth_reach = length // 32
    window_span = 2 * half_width + 1
    lag_count = length // 4
    forward = fourier_table(length)
    band_matrix = band_table(freq_count, smooth_reach)
    pieces = lax.all_to_all(records, "chan", split_axis=2, concat_axis=1, tiled=True)
    padded = jnp.pad(pieces, ((0, 0), (half_width, half_width), (0, 0)))
    amplitude = running_level(padded, length, window_span)
    whiten_pieces = pieces / jnp.maximum(amplitude, AMPLITUDE_FLOOR)
    spectrum = jnp.einsum("kt,wtc->wkc", forward, whiten_pieces, precision=HIGHEST)
    real_part = spectrum[:, :freq_count]
    imag_part = spectrum[:, freq_count:]
    magnitude = jnp.sqrt(real_part * real_part + imag_part * imag_part)
    smoothed = (
        jnp.einsum("jk,wkc->wjc", band_matrix, magnitude, precision=HIGHEST)
        / (2 * smooth_reach + 1)
        + WHITE_EPSILON
    )
    whitened = jnp.stack([real_part / smoothed, imag_part / smoothed], axis=1)
    band_data = lax.all_to_all(whitened, "win", split_axis=2, concat_axis=0, tiled=True)
    total_windows = band_data.shape[0]
    band_count = band_data.shape[2]
    source_count = sources.shape[0]
    chan_index = lax.axis_index("chan")
    channel_ids = jnp.arange(chan_width, dtype=jnp.int32)
    per_device = source_count // chan_count
    owned_local = (
        lax.dynamic_slice_in_dim(sources, chan_index * per_device, per_device)
        - chan_index * chan_width
    )
    selector = (owned_local[:, None] == channel_ids[None, :]).astype(jnp.float32)
    chosen = jnp.einsum("sc,wafc->wafs", selector, band_data, precision=HIGHEST)
    spectra = lax.all_gather(chosen, "chan", axis=3, tiled=True)
    source_real = spectra[:, 0]
    source_imag = spectra[:, 1]
    white_real = band_data[:, 0]
    white_imag = band_data[:, 1]
    cross_real = jnp.einsum(
        "wfs,wfc->fsc", source_real, white_real, precision=HIGHEST
    ) + jnp.einsum("wfs,wfc->fsc", source_imag, white_imag, precision=HIGHEST)
    cross_imag = jnp.einsum(
        "wfs,wfc->fsc", source_real, white_imag, precision=HIGHEST
    ) - jnp.einsum("wfs,wfc->fsc", source_imag, white_real, precision=HIGHEST)
    stacked = jnp.stack([cross_real, cross_imag])
    factor = 1.0 / math.sqrt(total_windows * freq_count)
    band_start = lax.axis_index("win") * band_count
    band_table_part = inverse_table(length, lag_count, band_start, band_count, factor).reshape(
        lag_count, 2, band_count
    )
    return lax.psum_scatter(
        jnp.einsum("tak,aksc->stc", band_table_part, stacked, precision=HIGHEST),
        "win",
        scatter_dimension=0,
        tiled=True,
    )


LANES = 128
STAGES = 2
BF16 = jnp.bfloat16
F32 = jnp.float32
MESH = pl.DeviceIdType.MESH


def bin_order(freq_count):
    per = freq_count // 8
    pairs = ((0, 4), (1, 7), (2, 6), (3, 5))
    return np.concatenate([8 * np.arange(per) + m for pair in pairs for m in pair])


def split_table(table):
    high = table.astype(np.float32).astype(BF16)
    low = (table - high.astype(np.float64)).astype(np.float32).astype(BF16)
    return np.stack([high, low])


def forward_blocks(length, time):
    per = length // 16
    rows = np.arange(time)[:, None]
    blocks = []
    for first, second in ((0, 4), (1, 7), (2, 6), (3, 5)):
        angle1 = 2 * np.pi * ((8 * np.arange(per) + first)[None, :] * rows % length) / length
        angle2 = 2 * np.pi * ((8 * np.arange(per) + second)[None, :] * rows % length) / length
        c1, s1, c2, s2 = np.cos(angle1), np.sin(angle1), np.cos(angle2), np.sin(angle2)
        if first == 0:
            zero = np.zeros_like(c1)
            top = np.concatenate([c1, zero, -s1, zero], axis=1)
            low = np.concatenate([zero, c2, zero, -s2], axis=1)
        else:
            top = np.concatenate([c1, c2, -s1, -s2], axis=1)
            low = np.concatenate([s1, -s2, c1, -c2], axis=1)
        blocks.append(np.concatenate([top, low], axis=0))
    return split_table(np.stack(blocks))


def smooth_table(freq_count, reach):
    order = bin_order(freq_count)
    return (np.abs(order[:, None] - order[None, :]) <= reach).astype(np.float32).astype(BF16)


def lag_table(length, lag_count, factor):
    bins = bin_order(length // 2)[:, None]
    lags = (np.arange(lag_count) - lag_count // 2)[None, :]
    angle = 2 * np.pi * (bins * lags % length) / length
    weight = np.where(bins == 0, 1.0, 2.0) * factor
    return split_table(np.concatenate([weight * np.cos(angle), -weight * np.sin(angle)], axis=0))


def halves(value):
    high = value.astype(BF16)
    return high, (value - high.astype(F32)).astype(BF16)


def stacked(value):
    return jnp.concatenate(halves(value), axis=0)


def dot(a, b):
    return jnp.dot(a, b, preferred_element_type=F32)


def folded(product):
    half = product.shape[0] // 2
    return product[:half] + product[half:]


def fused_kernel(
    half_width, smooth_reach, chan_count, win_count,
    src_hbm, rec_hbm, fwd_hbm, band_hbm, lag_hbm, out_ref,
    src_ref, rec, xt, recv, nrm, yy, fr, fi, mm, wr, wi, gs, cc, part, land,
    fwd, band, lag,
    rec_sem, tab_sem, a_send, a_recv, g_send, g_recv, r_send, r_recv,
):
    me = lax.axis_index("chan")
    row = lax.axis_index("win")
    windows, time, _ = rec.shape
    sets = 2 * windows
    group = xt.shape[2] // windows
    rows = sets * group
    width = STAGES * group
    freq = wr.shape[1]
    tiles = freq // LANES
    core, x, y = lax.rem(me, 2), lax.rem(me // 2, 2), me // 4
    upper, side = row // 2, lax.rem(row, 2)
    place = 2 * side + y
    far = (1 - upper, upper)
    column = [4 * far[s] + lax.rem(me, 4) for s in range(STAGES)]

    def flip(bit, by):
        return bit + by * (1 - 2 * bit)

    def masked(mask):
        dx, dy, z = mask >> 1 & 1, mask >> 2 & 1, mask >> 3
        chan = 4 * flip(y, dy) + 2 * flip(x, dx) + flip(core, mask & 1)
        return chan, row + z * (1 - 2 * side)

    def slot_of(chan, win):
        return lax.rem(win, 2) * chan_count + chan

    mine = slot_of(me, row)
    loads = [
        pltpu.make_async_copy(rec_hbm.at[w], rec.at[w], rec_sem.at[w]) for w in range(windows)
    ]
    tables = [
        pltpu.make_async_copy(hbm, vmem, tab_sem.at[i])
        for i, (hbm, vmem) in enumerate(
            ((fwd_hbm, fwd), (band_hbm, band), (lag_hbm, lag), (src_hbm, src_ref))
        )
    ]
    for copy in loads:
        copy.start()
    barrier = pltpu.get_barrier_semaphore()
    for mask in range(1, 2 * chan_count):
        chan, win = masked(mask)
        pl.semaphore_signal(
            barrier, inc=1, device_id={"chan": chan, "win": win}, device_id_type=MESH
        )
    for s in range(STAGES):
        for k in range(2):
            pl.semaphore_signal(
                barrier, inc=1, device_id={"chan": column[s], "win": 2 * (1 - upper) + k},
                device_id_type=MESH,
            )

    for copy in tables:
        copy.start()
    for w in range(windows):
        loads[w].wait()
        for h in range(2):
            tile = rec[w, :, h * LANES : (h + 1) * LANES].T
            for i in range(LANES // group):
                slot = i % 4 // 2 * chan_count + i % 2 * 4 + i // 4
                xt[h, slot, w * group : (w + 1) * group] = tile[i * group : (i + 1) * group]

    pl.semaphore_wait(barrier, 2 * chan_count - 1 + 2 * STAGES)

    for s in range(STAGES):
        for mask in (14, 15, 12, 13, 10, 11, 6, 7, 8, 9, 4, 5, 2, 3, 1):
            chan, win = masked(mask)
            pltpu.make_async_remote_copy(
                src_ref=xt.at[far[s], slot_of(chan, win)], dst_ref=recv.at[s, me, side],
                send_sem=a_send.at[s], recv_sem=a_recv.at[s],
                device_id={"chan": chan, "win": win}, device_id_type=MESH,
            ).start()
        pltpu.make_async_copy(xt.at[far[s], mine], recv.at[s, me, side], a_recv.at[s]).start()
    near_row = lax.broadcasted_iota(jnp.int32, (3 * time, time), 0) - time
    near_col = lax.broadcasted_iota(jnp.int32, (3 * time, time), 1)
    near = (jnp.abs(near_row - near_col) <= half_width).astype(F32).astype(BF16)
    root = math.sqrt(0.5)

    def settle(ref, sem):
        pltpu.make_async_copy(ref, ref, sem).wait()

    def normalise(s):
        for i in range(8):
            level = jnp.zeros((rows, time), F32)
            for j in range(max(i - 1, 0), min(i + 1, 7) + 1):
                both = stacked(jnp.abs(recv[s, j].reshape(rows, time)))
                level = level + folded(dot(both, near[(j - i + 1) * time : (j - i + 2) * time]))
            level = level * (1.0 / (2 * half_width + 1))
            nrm[i] = recv[s, i].reshape(rows, time) / jnp.maximum(level, AMPLITUDE_FLOOR)

    def butterfly(block, _):
        at = pl.ds(pl.multiple_of(block * 16, 16), 16)
        low_at = pl.ds(pl.multiple_of(rows + block * 16, 16), 16)
        n = [nrm[i, at, :] for i in range(8)]
        a = [n[i] + n[i + 4] for i in range(4)]
        b = [n[i] - n[i + 4] for i in range(4)]
        even, odd = a[0] + a[2], a[1] + a[3]
        diff, total = root * (b[1] - b[3]), root * (b[1] + b[3])
        pairs = (
            (even + odd, even - odd),
            (b[0] + diff, -(b[2] + total)),
            (a[0] - a[2], a[3] - a[1]),
            (b[0] - diff, b[2] - total),
        )
        for g, pair in enumerate(pairs):
            for k, value in enumerate(pair):
                high, low = halves(value)
                yy[g, at, k * time : (k + 1) * time] = high
                yy[g, low_at, k * time : (k + 1) * time] = low
        return 0

    def transform(s):
        lax.fori_loop(0, rows // 16, butterfly, 0)
        if s == 0:
            tables[0].wait()
        for g in range(4):
            at = slice(g * LANES, (g + 1) * LANES)
            both = folded(dot(yy[g], fwd[0, g])) + dot(yy[g, :rows], fwd[1, g])
            real, imag = both[:, :LANES], both[:, LANES:]
            fr[:, at] = real
            fi[:, at] = imag
            mm[:, at] = stacked(jnp.sqrt(real * real + imag * imag))

    def whiten(s):
        if s == 0:
            tables[1].wait()
        for g in range(freq // 256):
            at = slice(g * 256, (g + 1) * 256)
            smoothed = folded(dot(mm[...], band[:, at])) / (2 * smooth_reach + 1) + WHITE_EPSILON
            inverse = 1.0 / smoothed
            real, imag = fr[:, at] * inverse, fi[:, at] * inverse
            for w in range(sets):
                to = slice(w * width + s * group, w * width + (s + 1) * group)
                wr[to, at] = real[w * group : (w + 1) * group]
                wi[to, at] = imag[w * group : (w + 1) * group]

    def pick(s):
        if s == 0:
            tables[3].wait()
        owned = s * group + lax.rem(src_ref[4 * column[s] + place], group)
        for w in range(sets):
            gs[s, mine, 2 * w : 2 * w + 1, :] = wr[pl.ds(w * width + owned, 1), :]
            gs[s, mine, 2 * w + 1 : 2 * w + 2, :] = wi[pl.ds(w * width + owned, 1), :]

    def passing(s, block, target):
        mask = block ^ target
        chan, win = masked(target)
        slot = gs.at[s, slot_of(*masked(block))]
        return pltpu.make_async_remote_copy(
            src_ref=slot, dst_ref=slot, send_sem=g_send.at[s], recv_sem=g_recv.at[s, mask],
            device_id={"chan": chan, "win": win}, device_id_type=MESH,
        )

    gather = []
    for s in range(STAGES):
        moves = [passing(s, 0, target) for target in (1, 2, 4, 6, 8, 9)]
        moves += [passing(s, 8, target) for target in (2, 4, 6)]
        moves += [passing(s, block, 1) for block in (2, 4, 6, 10, 12, 14)]
        order = (1, 2, 4, 6, 8, 9, 10, 12, 14, 3, 5, 7, 11, 13, 15)
        gather.append(dict(zip(order, moves)))

    def relay(s, arrived, sent):
        for mask in arrived:
            gather[s][mask].wait_recv()
        for mask in sent:
            gather[s][mask].start()

    for s in range(STAGES):
        settle(recv.at[s], a_recv.at[s])
        normalise(s)
        transform(s)
        whiten(s)
        pick(s)
        if s == 0:
            relay(0, (), (8, 9, 1, 2, 4, 6))
    tables[2].wait()

    def compute(s, slots):
        count = len(slots)
        for t in range(tiles):
            at = slice(t * LANES, (t + 1) * LANES)
            sums = {}
            for w in range(sets):
                white = [
                    (wr[v : v + group, at], wi[v : v + group, at])
                    for v in range(w * width, (w + 1) * width, group)
                ]
                for j in range(count):
                    sr = gs[s, slots[j], 2 * w : 2 * w + 1, at]
                    si = gs[s, slots[j], 2 * w + 1 : 2 * w + 2, at]
                    for v in range(STAGES):
                        real, imag = white[v]
                        new = (sr * real + si * imag, sr * imag - si * real)
                        for k in range(2):
                            key = v, j, k
                            sums[key] = new[k] if w == 0 else sums[key] + new[k]
            for v in range(STAGES):
                for j in range(0, count, 2):
                    for k in range(2):
                        both = jnp.concatenate([sums[v, j, k], sums[v, j + 1, k]], axis=0)
                        high, low = halves(both)
                        col = k * freq + t * LANES
                        to = (v * count + j) * group
                        cc[to : to + 2 * group, col : col + LANES] = high
                        to = to + count * width
                        cc[to : to + 2 * group, col : col + LANES] = low
        half = count * width
        return folded(dot(cc[: 2 * half], lag[0])) + dot(cc[:half], lag[1])

    def deliver(q, v, owner, there, first, count, value):
        at = pl.ds(pl.multiple_of(first, 2 * group), count * group)
        here = (owner == row) & (column[v] == me)

        @pl.when(here)
        def _():
            land[upper, place, there, at] = value

        @pl.when(jnp.logical_not(here))
        def _():
            part[q, v, at] = value
            pltpu.make_async_remote_copy(
                src_ref=part.at[q, v, at], dst_ref=land.at[upper, place, there, at],
                send_sem=r_send.at[0], recv_sem=r_recv.at[0],
                device_id={"win": owner, "chan": column[v]}, device_id_type=MESH,
            ).start()

    def await_source(s, mask):
        pltpu.make_async_remote_copy(
            src_ref=gs.at[0, mine], dst_ref=gs.at[0, mine],
            send_sem=g_send.at[s], recv_sem=g_recv.at[s, mask],
            device_id={"chan": flip(core, 1) + me - core}, device_id_type=MESH,
        ).wait_recv()

    for z, mask in enumerate((1, 9)):
        if z == 1:
            relay(0, (8,), (10, 12, 14))
            relay(1, (), (8, 9, 1, 2, 4, 6))
        await_source(0, mask)
        line = flip(side, z)
        base = line * chan_count + 4 * y + 2 * x
        result = compute(0, (base, base + 1))
        for v in range(STAGES):
            value = result[2 * group * v : 2 * group * (v + 1)]
            deliver(0, v, 2 * far[0] + x, y, line * 2 * group, 2, value)

    def step(q, _):
        s, p = q // 4, lax.rem(q, 4)
        cross, later = lax.rem(p, 2), p // 2
        second = p * (3 - p) * (2 - p) // 2
        third = p * (p - 1) * (3 - p) // 2
        last = p * (p - 1) * (p - 2) // 6

        @pl.when(q == 1)
        def _():
            relay(0, (2, 6, 4), (3, 7, 5))

        @pl.when(q == 2)
        def _():
            relay(0, (12, 10), (13, 11))

        @pl.when(q == 3)
        def _():
            relay(0, (14,), (15,))
            relay(1, (8,), (10, 12, 14))

        @pl.when(q == 4)
        def _():
            relay(1, (2, 6, 4), (3, 7, 5))

        @pl.when(q == 5)
        def _():
            relay(1, (12, 10), (13, 11))

        @pl.when(q == 6)
        def _():
            relay(1, (14,), (15,))

        await_source(s, 1 + 2 * p + 4 * last)
        await_source(s, 9 - 2 * second + 4 * third + 6 * last)
        there = (1 - cross) * flip(y, later) + cross * flip(side, later)
        owner = 2 * (far[0] + s * (far[1] - far[0])) + flip(x, cross)
        slots = []
        for j in range(4):
            b, k = j // 2, j % 2
            r = (1 - cross) * b + cross * there
            at_y = (1 - cross) * there + cross * b
            slots.append(r * chan_count + 4 * at_y + 2 * flip(x, cross) + k)
        result = compute(s, slots)
        for v in range(STAGES):
            value = result[4 * group * v : 4 * group * (v + 1)]
            deliver(q, v, owner, there, 0, 4, value)
        return 0

    lax.fori_loop(1, STAGES * win_count, step, 0)

    settle(part.at[: STAGES * win_count - 1], r_recv.at[0])
    cross = side + x - 2 * side * x
    for there in range(2):
        for g in range(4):
            for j in range(4):
                b, k = j // 2, j % 2
                at = slice(j * group, (j + 1) * group)
                source = 4 * k + (1 - cross) * (2 * b + there) + cross * (b + 2 * there)
                to = pl.ds(pl.multiple_of((4 * source + g) * group, group), group)
                out_ref[to, :] = land[0, g, there, at] + land[1, g, there, at]

    for s in range(STAGES):
        settle(xt.at[s, : 2 * chan_count - 1], a_send.at[s])
        settle(gs.at[s, : 2 * chan_count - 1], g_send.at[s])
    settle(part.at[: STAGES * win_count - 1], r_send.at[0])


def fused(records, sources):
    chan_count, win_count = lax.axis_size("chan"), lax.axis_size("win")
    windows, time, channels = records.shape
    length = time * chan_count
    freq = length // 2
    group = channels // chan_count // 4
    sets = 2 * windows
    rows = sets * group
    source_count = sources.shape[0]
    lag_count = length // 4
    reach = length // 32
    half_width = min(16, time)
    owned = source_count // win_count
    factor = 1.0 / math.sqrt(windows * win_count * freq)
    fwd = forward_blocks(length, time)
    band = smooth_table(freq, reach)
    lag = lag_table(length, lag_count, factor)
    width = STAGES * group
    block = owned * 2 * width
    vmem = pl.BlockSpec(memory_space=pltpu.VMEM)
    hbm = pl.BlockSpec(memory_space=pltpu.HBM)
    dma = pltpu.SemaphoreType.DMA
    out = pl.pallas_call(
        functools.partial(fused_kernel, half_width, reach, chan_count, win_count),
        out_shape=pltpu.VMEM((block, lag_count), F32),
        in_specs=[hbm] * 5,
        out_specs=vmem,
        scratch_shapes=[
            pltpu.SMEM(sources.shape, jnp.int32),
            pltpu.VMEM(records.shape, F32),
            pltpu.VMEM((2, 2 * chan_count, windows * group, time), F32),
            pltpu.VMEM((STAGES, chan_count, 2, windows * group, time), F32),
            pltpu.VMEM((chan_count, rows, time), F32),
            pltpu.VMEM((4, 2 * rows, 2 * time), BF16),
            pltpu.VMEM((rows, freq), F32),
            pltpu.VMEM((rows, freq), F32),
            pltpu.VMEM((2 * rows, freq), BF16),
            pltpu.VMEM((sets * width, freq), F32),
            pltpu.VMEM((sets * width, freq), F32),
            pltpu.VMEM((STAGES, 2 * chan_count, 2 * sets, freq), F32),
            pltpu.VMEM((8 * width, 2 * freq), BF16),
            pltpu.VMEM((STAGES * win_count, STAGES, 4 * group, lag_count), F32),
            pltpu.VMEM((2, 4, 2, 4 * group, lag_count), F32),
            pltpu.VMEM(fwd.shape, BF16),
            pltpu.VMEM(band.shape, BF16),
            pltpu.VMEM(lag.shape, BF16),
            dma((windows,)),
            dma((4,)),
            dma((STAGES,)),
            dma((STAGES,)),
            dma((STAGES,)),
            dma((STAGES, 2 * chan_count)),
            dma((1,)),
            dma((1,)),
        ],
        compiler_params=pltpu.CompilerParams(
            collective_id=0, has_side_effects=True, vmem_limit_bytes=40_000_000
        ),
        name="interferometry",
    )(*[
        pltpu.with_memory_space_constraint(value, pltpu.HBM)
        for value in (sources, records, jnp.asarray(fwd), jnp.asarray(band), jnp.asarray(lag))
    ])
    return out.reshape(owned, 2 * width, lag_count).transpose(0, 2, 1)


def fits(records, sources):
    chan_count, win_count = lax.axis_size("chan"), lax.axis_size("win")
    windows, time, channels = records.shape
    return (
        time == LANES and chan_count == 8 and win_count == 4 and channels % LANES == 0
        and channels == 32 * chan_count and sources.shape[0] == 4 * chan_count
        and windows % 2 == 0
    )


def body(records, sources):
    return fused(records, sources) if fits(records, sources) else local(records, sources)


def solution(mesh):
    placed = (P("win", "chan", None), P())
    return jax.shard_map(
        body, mesh=mesh, in_specs=placed, out_specs=P("win", None, "chan"), check_vma=False
    )
```

```python
import functools
import math

import jax
import jax.numpy as jnp
import numpy as np
from jax import lax
from jax.experimental import pallas as pl
from jax.experimental.pallas import tpu as pltpu
from jax.sharding import PartitionSpec as P

HIGHEST = lax.Precision.HIGHEST
AMPLITUDE_FLOOR = 0.25
WHITE_EPSILON = 1e-06


def fourier_table(length):
    freq_count = length // 2
    freqs = jnp.arange(freq_count, dtype=jnp.int32)[:, None]
    sample_index = jnp.arange(length, dtype=jnp.int32)[None, :]
    angles = (freqs * sample_index % length).astype(jnp.float32) * (2.0 * math.pi / length)
    return jnp.concatenate([jnp.cos(angles), -jnp.sin(angles)], axis=0)


def band_table(freq_count, reach):
    rows_index = jnp.arange(freq_count, dtype=jnp.int32)[:, None]
    cols_index = jnp.arange(freq_count, dtype=jnp.int32)[None, :]
    return (jnp.abs(rows_index - cols_index) <= reach).astype(jnp.float32)


def inverse_table(length, lag_count, first_bin, bin_count, factor):
    freqs = first_bin + jnp.arange(bin_count, dtype=jnp.int32)
    lag_index = jnp.arange(lag_count, dtype=jnp.int32) - lag_count // 2
    angles = (lag_index[:, None] * freqs[None, :] % length).astype(jnp.float32) * (
        2.0 * math.pi / length
    )
    weights = jnp.where(freqs == 0, 1.0, 2.0).astype(jnp.float32)[None, :] * factor
    return jnp.concatenate([weights * jnp.cos(angles), -weights * jnp.sin(angles)], axis=1)


def running_level(padded, time_count, window_span):
    window_total = padded.shape[0]
    chans = padded.shape[2]
    running = jnp.concatenate(
        [jnp.zeros((window_total, 1, chans), jnp.float32), jnp.cumsum(jnp.abs(padded), axis=1)],
        axis=1,
    )
    return (running[:, window_span:] - running[:, :time_count]) / window_span


def local(records, sources):
    chan_count = lax.axis_size("chan")
    local_windows, local_time, all_channels = records.shape
    length = local_time * chan_count
    freq_count = length // 2
    chan_width = all_channels // chan_count
    half_width = min(16, local_time)
    smooth_reach = length // 32
    window_span = 2 * half_width + 1
    lag_count = length // 4
    forward = fourier_table(length)
    band_matrix = band_table(freq_count, smooth_reach)
    pieces = lax.all_to_all(records, "chan", split_axis=2, concat_axis=1, tiled=True)
    padded = jnp.pad(pieces, ((0, 0), (half_width, half_width), (0, 0)))
    amplitude = running_level(padded, length, window_span)
    whiten_pieces = pieces / jnp.maximum(amplitude, AMPLITUDE_FLOOR)
    spectrum = jnp.einsum("kt,wtc->wkc", forward, whiten_pieces, precision=HIGHEST)
    real_part = spectrum[:, :freq_count]
    imag_part = spectrum[:, freq_count:]
    magnitude = jnp.sqrt(real_part * real_part + imag_part * imag_part)
    smoothed = (
        jnp.einsum("jk,wkc->wjc", band_matrix, magnitude, precision=HIGHEST)
        / (2 * smooth_reach + 1)
        + WHITE_EPSILON
    )
    whitened = jnp.stack([real_part / smoothed, imag_part / smoothed], axis=1)
    band_data = lax.all_to_all(whitened, "win", split_axis=2, concat_axis=0, tiled=True)
    total_windows = band_data.shape[0]
    band_count = band_data.shape[2]
    source_count = sources.shape[0]
    chan_index = lax.axis_index("chan")
    channel_ids = jnp.arange(chan_width, dtype=jnp.int32)
    per_device = source_count // chan_count
    owned_local = (
        lax.dynamic_slice_in_dim(sources, chan_index * per_device, per_device)
        - chan_index * chan_width
    )
    selector = (owned_local[:, None] == channel_ids[None, :]).astype(jnp.float32)
    chosen = jnp.einsum("sc,wafc->wafs", selector, band_data, precision=HIGHEST)
    spectra = lax.all_gather(chosen, "chan", axis=3, tiled=True)
    source_real = spectra[:, 0]
    source_imag = spectra[:, 1]
    white_real = band_data[:, 0]
    white_imag = band_data[:, 1]
    cross_real = jnp.einsum(
        "wfs,wfc->fsc", source_real, white_real, precision=HIGHEST
    ) + jnp.einsum("wfs,wfc->fsc", source_imag, white_imag, precision=HIGHEST)
    cross_imag = jnp.einsum(
        "wfs,wfc->fsc", source_real, white_imag, precision=HIGHEST
    ) - jnp.einsum("wfs,wfc->fsc", source_imag, white_real, precision=HIGHEST)
    stacked = jnp.stack([cross_real, cross_imag])
    factor = 1.0 / math.sqrt(total_windows * freq_count)
    band_start = lax.axis_index("win") * band_count
    band_table_part = inverse_table(length, lag_count, band_start, band_count, factor).reshape(
        lag_count, 2, band_count
    )
    return lax.psum_scatter(
        jnp.einsum("tak,aksc->stc", band_table_part, stacked, precision=HIGHEST),
        "win",
        scatter_dimension=0,
        tiled=True,
    )


LANES = 128
STAGES = 2
BF16 = jnp.bfloat16
F32 = jnp.float32
MESH = pl.DeviceIdType.MESH


def bin_order(freq_count):
    per = freq_count // 8
    pairs = ((0, 4), (1, 7), (2, 6), (3, 5))
    return np.concatenate([8 * np.arange(per) + m for pair in pairs for m in pair])


def split_table(table):
    high = table.astype(np.float32).astype(BF16)
    low = (table - high.astype(np.float64)).astype(np.float32).astype(BF16)
    return np.stack([high, low])


def forward_blocks(length, time):
    per = length // 16
    rows = np.arange(time)[:, None]
    blocks = []
    for first, second in ((0, 4), (1, 7), (2, 6), (3, 5)):
        angle1 = 2 * np.pi * ((8 * np.arange(per) + first)[None, :] * rows % length) / length
        angle2 = 2 * np.pi * ((8 * np.arange(per) + second)[None, :] * rows % length) / length
        c1, s1, c2, s2 = np.cos(angle1), np.sin(angle1), np.cos(angle2), np.sin(angle2)
        if first == 0:
            zero = np.zeros_like(c1)
            top = np.concatenate([c1, zero, -s1, zero], axis=1)
            low = np.concatenate([zero, c2, zero, -s2], axis=1)
        else:
            top = np.concatenate([c1, c2, -s1, -s2], axis=1)
            low = np.concatenate([s1, -s2, c1, -c2], axis=1)
        blocks.append(np.concatenate([top, low], axis=0))
    return split_table(np.stack(blocks))


def smooth_table(freq_count, reach):
    order = bin_order(freq_count)
    return (np.abs(order[:, None] - order[None, :]) <= reach).astype(np.float32).astype(BF16)


def lag_table(length, lag_count, factor):
    bins = bin_order(length // 2)[:, None]
    lags = (np.arange(lag_count) - lag_count // 2)[None, :]
    angle = 2 * np.pi * (bins * lags % length) / length
    weight = np.where(bins == 0, 1.0, 2.0) * factor
    return split_table(np.concatenate([weight * np.cos(angle), -weight * np.sin(angle)], axis=0))


def halves(value):
    high = value.astype(BF16)
    return high, (value - high.astype(F32)).astype(BF16)


def stacked(value):
    return jnp.concatenate(halves(value), axis=0)


def dot(a, b):
    return jnp.dot(a, b, preferred_element_type=F32)


def folded(product):
    half = product.shape[0] // 2
    return product[:half] + product[half:]


def fused_kernel(
    half_width, smooth_reach, chan_count, win_count,
    src_hbm, rec_hbm, fwd_hbm, band_hbm, lag_hbm, out_ref,
    src_ref, rec, xt, recv, nrm, yy, fr, fi, mm, ww, wo, gs, cc, part, land,
    fwd, band, lag,
    rec_sem, tab_sem, a_send, a_recv, g_send, g_recv, w_send, w_recv, r_send, r_recv,
):
    me = lax.axis_index("chan")
    row = lax.axis_index("win")
    windows, time, _ = rec.shape
    sets = 2 * windows
    group = xt.shape[2] // windows
    rows = sets * group
    freq = fr.shape[1]
    tiles = freq // LANES
    core, x, y = lax.rem(me, 2), lax.rem(me // 2, 2), me // 4
    upper, side = row // 2, lax.rem(row, 2)
    place = 2 * side + y
    far = (1 - upper, upper)
    column = [4 * far[s] + lax.rem(me, 4) for s in range(STAGES)]

    def flip(bit, by):
        return bit + by * (1 - 2 * bit)

    def masked(mask):
        dx, dy, z = mask >> 1 & 1, mask >> 2 & 1, mask >> 3
        chan = 4 * flip(y, dy) + 2 * flip(x, dx) + flip(core, mask & 1)
        return chan, row + z * (1 - 2 * side)

    def slot_of(chan, win):
        return lax.rem(win, 2) * chan_count + chan

    mine = slot_of(me, row)
    loads = [
        pltpu.make_async_copy(rec_hbm.at[w], rec.at[w], rec_sem.at[w]) for w in range(windows)
    ]
    tables = [
        pltpu.make_async_copy(hbm, vmem, tab_sem.at[i])
        for i, (hbm, vmem) in enumerate(
            ((fwd_hbm, fwd), (band_hbm, band), (lag_hbm, lag), (src_hbm, src_ref))
        )
    ]
    for copy in loads:
        copy.start()
    barrier = pltpu.get_barrier_semaphore()
    for mask in range(1, 2 * chan_count):
        chan, win = masked(mask)
        pl.semaphore_signal(
            barrier, inc=1, device_id={"chan": chan, "win": win}, device_id_type=MESH
        )
    for s in range(STAGES):
        for k in range(2):
            pl.semaphore_signal(
                barrier, inc=1, device_id={"chan": column[s], "win": 2 * (1 - upper) + k},
                device_id_type=MESH,
            )

    for copy in tables:
        copy.start()
    for w in range(windows):
        loads[w].wait()
        for h in range(2):
            tile = rec[w, :, h * LANES : (h + 1) * LANES].T
            for i in range(LANES // group):
                slot = i % 4 // 2 * chan_count + i % 2 * 4 + i // 4
                xt[h, slot, w * group : (w + 1) * group] = tile[i * group : (i + 1) * group]

    pl.semaphore_wait(barrier, 2 * chan_count - 1 + 2 * STAGES)

    for s in range(STAGES):
        for mask in (14, 15, 12, 13, 10, 11, 6, 7, 8, 9, 4, 5, 2, 3, 1):
            chan, win = masked(mask)
            pltpu.make_async_remote_copy(
                src_ref=xt.at[far[s], slot_of(chan, win)], dst_ref=recv.at[s, me, side],
                send_sem=a_send.at[s], recv_sem=a_recv.at[s],
                device_id={"chan": chan, "win": win}, device_id_type=MESH,
            ).start()
        pltpu.make_async_copy(xt.at[far[s], mine], recv.at[s, me, side], a_recv.at[s]).start()
    near_row = lax.broadcasted_iota(jnp.int32, (3 * time, time), 0) - time
    near_col = lax.broadcasted_iota(jnp.int32, (3 * time, time), 1)
    near = (jnp.abs(near_row - near_col) <= half_width).astype(F32).astype(BF16)
    root = math.sqrt(0.5)

    def settle(ref, sem):
        pltpu.make_async_copy(ref, ref, sem).wait()

    def normalise(s):
        for i in range(8):
            level = jnp.zeros((rows, time), F32)
            for j in range(max(i - 1, 0), min(i + 1, 7) + 1):
                both = stacked(jnp.abs(recv[s, j].reshape(rows, time)))
                level = level + folded(dot(both, near[(j - i + 1) * time : (j - i + 2) * time]))
            level = level * (1.0 / (2 * half_width + 1))
            nrm[i] = recv[s, i].reshape(rows, time) / jnp.maximum(level, AMPLITUDE_FLOOR)

    def butterfly(block, _):
        at = pl.ds(pl.multiple_of(block * 16, 16), 16)
        low_at = pl.ds(pl.multiple_of(rows + block * 16, 16), 16)
        n = [nrm[i, at, :] for i in range(8)]
        a = [n[i] + n[i + 4] for i in range(4)]
        b = [n[i] - n[i + 4] for i in range(4)]
        even, odd = a[0] + a[2], a[1] + a[3]
        diff, total = root * (b[1] - b[3]), root * (b[1] + b[3])
        pairs = (
            (even + odd, even - odd),
            (b[0] + diff, -(b[2] + total)),
            (a[0] - a[2], a[3] - a[1]),
            (b[0] - diff, b[2] - total),
        )
        for g, pair in enumerate(pairs):
            for k, value in enumerate(pair):
                high, low = halves(value)
                yy[g, at, k * time : (k + 1) * time] = high
                yy[g, low_at, k * time : (k + 1) * time] = low
        return 0

    def transform(s):
        lax.fori_loop(0, rows // 16, butterfly, 0)
        if s == 0:
            tables[0].wait()
        for g in range(4):
            at = slice(g * LANES, (g + 1) * LANES)
            both = folded(dot(yy[g], fwd[0, g])) + dot(yy[g, :rows], fwd[1, g])
            real, imag = both[:, :LANES], both[:, LANES:]
            fr[:, at] = real
            fi[:, at] = imag
            mm[:, at] = stacked(jnp.sqrt(real * real + imag * imag))

    def whiten(s):
        if s == 0:
            tables[1].wait()
        for g in range(freq // 256):
            at = slice(g * 256, (g + 1) * 256)
            smoothed = folded(dot(mm[...], band[:, at])) / (2 * smooth_reach + 1) + WHITE_EPSILON
            inverse = 1.0 / smoothed
            ww[s, 0, :, at] = fr[:, at] * inverse
            ww[s, 1, :, at] = fi[:, at] * inverse

    def pick(s):
        if s == 0:
            tables[3].wait()
        owned = lax.rem(src_ref[4 * column[s] + place], group)
        for w in range(sets):
            for k in range(2):
                line = 2 * w + k
                gs[s, mine, line : line + 1, :] = ww[s, k, pl.ds(w * group + owned, 1), :]

    def offer(s, mask):
        chan, win = masked(mask)
        return pltpu.make_async_remote_copy(
            src_ref=gs.at[s, mine], dst_ref=gs.at[s, mine],
            send_sem=g_send.at[s], recv_sem=g_recv.at[s, mask],
            device_id={"chan": chan, "win": win}, device_id_type=MESH,
        )

    def offers(s, masks):
        for mask in masks:
            offer(s, mask).start()

    def arrive(s, masks):
        for mask in masks:
            offer(s, mask).wait_recv()

    def share(s):
        chan, win = masked(1)
        return pltpu.make_async_remote_copy(
            src_ref=ww.at[s], dst_ref=wo.at[s],
            send_sem=w_send.at[s], recv_sem=w_recv.at[s],
            device_id={"chan": chan, "win": win}, device_id_type=MESH,
        )

    for s in range(STAGES):
        settle(recv.at[s], a_recv.at[s])
        if s == 1:
            offers(0, (6, 12, 10, 14))
        normalise(s)
        transform(s)
        whiten(s)
        share(s).start()
        pick(s)
        offers(s, ((1, 2, 4, 8), (2, 4, 8))[s])
    tables[2].wait()

    def compute(sources, entries):
        half = len(entries) * group
        targets = sorted({target for _, target in entries})
        for t in range(tiles):
            at = slice(t * LANES, (t + 1) * LANES)
            sums = {}
            for w in range(sets):
                rows_at = slice(w * group, (w + 1) * group)
                white = {
                    (j, v): tuple((ww, wo)[j][v, k, rows_at, at] for k in range(2))
                    for j, v in targets
                }
                lines = [
                    (gs[s, slot, 2 * w : 2 * w + 1, at], gs[s, slot, 2 * w + 1 : 2 * w + 2, at])
                    for s, slot in sources
                ]
                for n, (source, target) in enumerate(entries):
                    (sr, si), (real, imag) = lines[source], white[target]
                    new = (sr * real + si * imag, sr * imag - si * real)
                    for k in range(2):
                        sums[n, k] = new[k] if w == 0 else sums[n, k] + new[k]
            for n in range(0, len(entries), 2):
                for k in range(2):
                    high, low = halves(jnp.concatenate([sums[n, k], sums[n + 1, k]], axis=0))
                    col = k * freq + t * LANES
                    cc[n * group : (n + 2) * group, col : col + LANES] = high
                    cc[half + n * group : half + (n + 2) * group, col : col + LANES] = low
        return folded(dot(cc[: 2 * half], lag[0])) + dot(cc[:half], lag[1])

    def deliver(staged, landed, j, v, owner, value):
        def send():
            staged[...] = value
            pltpu.make_async_remote_copy(
                src_ref=staged, dst_ref=landed, send_sem=r_send.at[0], recv_sem=r_recv.at[0],
                device_id={"win": owner, "chan": column[v] + j * (1 - 2 * core)},
                device_id_type=MESH,
            ).start()

        if j == 1:
            send()
            return
        here = (owner == row) & (column[v] == me)

        @pl.when(here)
        def _():
            landed[...] = value

        @pl.when(jnp.logical_not(here))
        def _():
            send()

    steps = 2 * win_count - 1
    base = side * chan_count + 4 * y + 2 * x
    arrive(0, (1,))
    entries = [(k, (0, v)) for v in range(STAGES) for k in range(2)]
    result = compute([(0, base), (0, base + 1)], entries)
    for n, (k, (_, v)) in enumerate(entries):
        at = slice(n * group, (n + 1) * group)
        spot = pl.ds(pl.multiple_of(y * group, group), group)
        deliver(
            part.at[2 * steps, at], land.at[upper, place, side, k, spot], 0, v,
            2 * far[0] + x, result[at],
        )
    offers(1, (6,))
    for s in range(STAGES):
        share(s).wait_recv()
    arrive(0, (4,))
    entries = [(0, (j, v)) for j in range(2) for v in range(STAGES)]
    result = compute([(0, side * chan_count + 4 * (1 - y) + 2 * x + core)], entries)
    for n, (_, (j, v)) in enumerate(entries):
        at = slice(n * group, (n + 1) * group)
        spot = pl.ds(pl.multiple_of((1 - y) * group, group), group)
        deliver(
            part.at[2 * steps + 2, at], land.at[upper, place, side, core, spot], j, v,
            2 * far[0] + x, result[at],
        )

    def forward():
        arrive(1, (8,))
        for target in (2, 4, 6):
            chan, win = masked(target)
            slot = gs.at[1, slot_of(*masked(8))]
            pltpu.make_async_remote_copy(
                src_ref=slot, dst_ref=slot, send_sem=g_send.at[1], recv_sem=g_recv.at[1, 8 | target],
                device_id={"chan": chan, "win": win}, device_id_type=MESH,
            ).start()

    def step(q, _):
        s = (q + 1) // 4
        i = q - 3 * s
        e = flip(x, 1 - upper)
        early = (2 - i) * (1 - i) // 2 * (2 - e) + i * (2 - i) * (1 + 2 * e) + i * (i - 1) // 2 * (3 - e)
        t = (1 - s) * early + s * (2 * lax.rem(i, 2) + flip(i // 2, flip(x, upper)))
        at_x, r = flip(x, lax.rem(t, 2)), flip(side, t // 2)
        owner = 2 * (far[0] + s * (far[1] - far[0])) + at_x
        @pl.when(q == 1)
        def _():
            forward()

        for k, masks in enumerate(((4,), (2, 6), (8, 12), (10, 14))):
            for stage in range(1 - min(k, 1), STAGES):
                @pl.when((s == stage) & (t == k))
                def _():
                    arrive(stage, masks[stage:] if k == 2 else masks)

        slots = [(s, r * chan_count + 4 * there + 2 * at_x + core) for there in range(2)]
        entries = [(n, (j, v)) for j in range(2) for v in range(STAGES) for n in range(2)]
        result = compute(slots, entries)
        for j in (1, 0):
            for v in range(STAGES):
                first = (2 * j + v) * 2 * group
                deliver(
                    part.at[2 * q + j, v * 2 * group : (v + 1) * 2 * group],
                    land.at[upper, place, r, core], j, v, owner, result[first : first + 2 * group],
                )
        return 0

    lax.fori_loop(0, steps, step, 0)

    settle(part.at[: 2 * steps + 1], r_recv.at[0])
    for g in range(4):
        for r in range(2):
            for k in range(2):
                for there in range(2):
                    at = slice(there * group, (there + 1) * group)
                    to = ((4 * k + 2 * r + there) * 4 + g) * group
                    out_ref[to : to + group, :] = land[0, g, r, k, at] + land[1, g, r, k, at]

    for s in range(STAGES):
        settle(xt.at[s, : 2 * chan_count - 1], a_send.at[s])
        settle(gs.at[s, : 8 - s], g_send.at[s])
        settle(ww.at[s], w_send.at[s])
    settle(part.at[: 2 * steps + 1], r_send.at[0])


def fused(records, sources):
    chan_count, win_count = lax.axis_size("chan"), lax.axis_size("win")
    windows, time, channels = records.shape
    length = time * chan_count
    freq = length // 2
    group = channels // chan_count // 4
    sets = 2 * windows
    rows = sets * group
    source_count = sources.shape[0]
    lag_count = length // 4
    reach = length // 32
    half_width = min(16, time)
    owned = source_count // win_count
    factor = 1.0 / math.sqrt(windows * win_count * freq)
    fwd = forward_blocks(length, time)
    band = smooth_table(freq, reach)
    lag = lag_table(length, lag_count, factor)
    width = STAGES * group
    block = owned * 2 * width
    vmem = pl.BlockSpec(memory_space=pltpu.VMEM)
    hbm = pl.BlockSpec(memory_space=pltpu.HBM)
    dma = pltpu.SemaphoreType.DMA
    out = pl.pallas_call(
        functools.partial(fused_kernel, half_width, reach, chan_count, win_count),
        out_shape=pltpu.VMEM((block, lag_count), F32),
        in_specs=[hbm] * 5,
        out_specs=vmem,
        scratch_shapes=[
            pltpu.SMEM(sources.shape, jnp.int32),
            pltpu.VMEM(records.shape, F32),
            pltpu.VMEM((2, 2 * chan_count, windows * group, time), F32),
            pltpu.VMEM((STAGES, chan_count, 2, windows * group, time), F32),
            pltpu.VMEM((chan_count, rows, time), F32),
            pltpu.VMEM((4, 2 * rows, 2 * time), BF16),
            pltpu.VMEM((rows, freq), F32),
            pltpu.VMEM((rows, freq), F32),
            pltpu.VMEM((2 * rows, freq), BF16),
            pltpu.VMEM((STAGES, 2, rows, freq), F32),
            pltpu.VMEM((STAGES, 2, rows, freq), F32),
            pltpu.VMEM((STAGES, 2 * chan_count, 2 * sets, freq), F32),
            pltpu.VMEM((16 * group, 2 * freq), BF16),
            pltpu.VMEM((4 * win_count + 2, 4 * group, lag_count), F32),
            pltpu.VMEM((2, 4, 2, 2, 2 * group, lag_count), F32),
            pltpu.VMEM(fwd.shape, BF16),
            pltpu.VMEM(band.shape, BF16),
            pltpu.VMEM(lag.shape, BF16),
            dma((windows,)),
            dma((4,)),
            dma((STAGES,)),
            dma((STAGES,)),
            dma((STAGES,)),
            dma((STAGES, 2 * chan_count)),
            dma((STAGES,)),
            dma((STAGES,)),
            dma((1,)),
            dma((1,)),
        ],
        compiler_params=pltpu.CompilerParams(
            collective_id=0, has_side_effects=True, vmem_limit_bytes=40_000_000
        ),
        name="interferometry",
    )(*[
        pltpu.with_memory_space_constraint(value, pltpu.HBM)
        for value in (sources, records, jnp.asarray(fwd), jnp.asarray(band), jnp.asarray(lag))
    ])
    return out.reshape(owned, 2 * width, lag_count).transpose(0, 2, 1)


def fits(records, sources):
    chan_count, win_count = lax.axis_size("chan"), lax.axis_size("win")
    windows, time, channels = records.shape
    return (
        time == LANES and chan_count == 8 and win_count == 4 and channels % LANES == 0
        and channels == 32 * chan_count and sources.shape[0] == 4 * chan_count
        and windows % 2 == 0
    )


def body(records, sources):
    return fused(records, sources) if fits(records, sources) else local(records, sources)


def solution(mesh):
    placed = (P("win", "chan", None), P())
    return jax.shard_map(
        body, mesh=mesh, in_specs=placed, out_specs=P("win", None, "chan"), check_vma=False
    )
```

```python
import functools
import math

import jax
import jax.numpy as jnp
import numpy as np
from jax import lax
from jax.experimental import pallas as pl
from jax.experimental.pallas import tpu as pltpu
from jax.sharding import PartitionSpec as P

HIGHEST = lax.Precision.HIGHEST
AMPLITUDE_FLOOR = 0.25
WHITE_EPSILON = 1e-06


def fourier_table(length):
    freq_count = length // 2
    freqs = jnp.arange(freq_count, dtype=jnp.int32)[:, None]
    sample_index = jnp.arange(length, dtype=jnp.int32)[None, :]
    angles = (freqs * sample_index % length).astype(jnp.float32) * (2.0 * math.pi / length)
    return jnp.concatenate([jnp.cos(angles), -jnp.sin(angles)], axis=0)


def band_table(freq_count, reach):
    rows_index = jnp.arange(freq_count, dtype=jnp.int32)[:, None]
    cols_index = jnp.arange(freq_count, dtype=jnp.int32)[None, :]
    return (jnp.abs(rows_index - cols_index) <= reach).astype(jnp.float32)


def inverse_table(length, lag_count, first_bin, bin_count, factor):
    freqs = first_bin + jnp.arange(bin_count, dtype=jnp.int32)
    lag_index = jnp.arange(lag_count, dtype=jnp.int32) - lag_count // 2
    angles = (lag_index[:, None] * freqs[None, :] % length).astype(jnp.float32) * (
        2.0 * math.pi / length
    )
    weights = jnp.where(freqs == 0, 1.0, 2.0).astype(jnp.float32)[None, :] * factor
    return jnp.concatenate([weights * jnp.cos(angles), -weights * jnp.sin(angles)], axis=1)


def running_level(padded, time_count, window_span):
    window_total = padded.shape[0]
    chans = padded.shape[2]
    running = jnp.concatenate(
        [jnp.zeros((window_total, 1, chans), jnp.float32), jnp.cumsum(jnp.abs(padded), axis=1)],
        axis=1,
    )
    return (running[:, window_span:] - running[:, :time_count]) / window_span


def local(records, sources):
    chan_count = lax.axis_size("chan")
    local_windows, local_time, all_channels = records.shape
    length = local_time * chan_count
    freq_count = length // 2
    chan_width = all_channels // chan_count
    half_width = min(16, local_time)
    smooth_reach = length // 32
    window_span = 2 * half_width + 1
    lag_count = length // 4
    forward = fourier_table(length)
    band_matrix = band_table(freq_count, smooth_reach)
    pieces = lax.all_to_all(records, "chan", split_axis=2, concat_axis=1, tiled=True)
    padded = jnp.pad(pieces, ((0, 0), (half_width, half_width), (0, 0)))
    amplitude = running_level(padded, length, window_span)
    whiten_pieces = pieces / jnp.maximum(amplitude, AMPLITUDE_FLOOR)
    spectrum = jnp.einsum("kt,wtc->wkc", forward, whiten_pieces, precision=HIGHEST)
    real_part = spectrum[:, :freq_count]
    imag_part = spectrum[:, freq_count:]
    magnitude = jnp.sqrt(real_part * real_part + imag_part * imag_part)
    smoothed = (
        jnp.einsum("jk,wkc->wjc", band_matrix, magnitude, precision=HIGHEST)
        / (2 * smooth_reach + 1)
        + WHITE_EPSILON
    )
    whitened = jnp.stack([real_part / smoothed, imag_part / smoothed], axis=1)
    band_data = lax.all_to_all(whitened, "win", split_axis=2, concat_axis=0, tiled=True)
    total_windows = band_data.shape[0]
    band_count = band_data.shape[2]
    source_count = sources.shape[0]
    chan_index = lax.axis_index("chan")
    channel_ids = jnp.arange(chan_width, dtype=jnp.int32)
    per_device = source_count // chan_count
    owned_local = (
        lax.dynamic_slice_in_dim(sources, chan_index * per_device, per_device)
        - chan_index * chan_width
    )
    selector = (owned_local[:, None] == channel_ids[None, :]).astype(jnp.float32)
    chosen = jnp.einsum("sc,wafc->wafs", selector, band_data, precision=HIGHEST)
    spectra = lax.all_gather(chosen, "chan", axis=3, tiled=True)
    source_real = spectra[:, 0]
    source_imag = spectra[:, 1]
    white_real = band_data[:, 0]
    white_imag = band_data[:, 1]
    cross_real = jnp.einsum(
        "wfs,wfc->fsc", source_real, white_real, precision=HIGHEST
    ) + jnp.einsum("wfs,wfc->fsc", source_imag, white_imag, precision=HIGHEST)
    cross_imag = jnp.einsum(
        "wfs,wfc->fsc", source_real, white_imag, precision=HIGHEST
    ) - jnp.einsum("wfs,wfc->fsc", source_imag, white_real, precision=HIGHEST)
    stacked = jnp.stack([cross_real, cross_imag])
    factor = 1.0 / math.sqrt(total_windows * freq_count)
    band_start = lax.axis_index("win") * band_count
    band_table_part = inverse_table(length, lag_count, band_start, band_count, factor).reshape(
        lag_count, 2, band_count
    )
    return lax.psum_scatter(
        jnp.einsum("tak,aksc->stc", band_table_part, stacked, precision=HIGHEST),
        "win",
        scatter_dimension=0,
        tiled=True,
    )


LANES = 128
STAGES = 2
BF16 = jnp.bfloat16
F32 = jnp.float32
MESH = pl.DeviceIdType.MESH


def bin_order(freq_count):
    per = freq_count // 8
    pairs = ((0, 4), (1, 7), (2, 6), (3, 5))
    return np.concatenate([8 * np.arange(per) + m for pair in pairs for m in pair])


def split_table(table):
    high = table.astype(np.float32).astype(BF16)
    low = (table - high.astype(np.float64)).astype(np.float32).astype(BF16)
    return np.stack([high, low])


def forward_blocks(length, time):
    per = length // 16
    rows = np.arange(time)[:, None]
    blocks = []
    for first, second in ((0, 4), (1, 7), (2, 6), (3, 5)):
        angle1 = 2 * np.pi * ((8 * np.arange(per) + first)[None, :] * rows % length) / length
        angle2 = 2 * np.pi * ((8 * np.arange(per) + second)[None, :] * rows % length) / length
        c1, s1, c2, s2 = np.cos(angle1), np.sin(angle1), np.cos(angle2), np.sin(angle2)
        if first == 0:
            zero = np.zeros_like(c1)
            top = np.concatenate([c1, zero, -s1, zero], axis=1)
            low = np.concatenate([zero, c2, zero, -s2], axis=1)
        else:
            top = np.concatenate([c1, c2, -s1, -s2], axis=1)
            low = np.concatenate([s1, -s2, c1, -c2], axis=1)
        blocks.append(np.concatenate([top, low], axis=0))
    return split_table(np.stack(blocks))


def smooth_table(freq_count, reach):
    order = bin_order(freq_count)
    return (np.abs(order[:, None] - order[None, :]) <= reach).astype(np.float32).astype(BF16)


def lag_table(length, lag_count, factor):
    bins = bin_order(length // 2)[:, None]
    lags = (np.arange(lag_count) - lag_count // 2)[None, :]
    angle = 2 * np.pi * (bins * lags % length) / length
    weight = np.where(bins == 0, 1.0, 2.0) * factor
    return split_table(np.concatenate([weight * np.cos(angle), -weight * np.sin(angle)], axis=0))


def halves(value):
    high = value.astype(BF16)
    return high, (value - high.astype(F32)).astype(BF16)


def stacked(value):
    return jnp.concatenate(halves(value), axis=0)


def dot(a, b):
    return jnp.dot(a, b, preferred_element_type=F32)


def folded(product):
    half = product.shape[0] // 2
    return product[:half] + product[half:]


def fused_kernel(
    half_width, smooth_reach, chan_count, win_count,
    src_hbm, rec_hbm, fwd_hbm, band_hbm, lag_hbm, out_ref,
    src_ref, rec, xt, recv, nrm, yy, fr, fi, mm, ww, wo, gs, cc, part, land,
    fwd, band, lag,
    rec_sem, tab_sem, sent, a_recv, g_recv, w_recv, r_recv,
):
    me = lax.axis_index("chan")
    row = lax.axis_index("win")
    windows, time, _ = rec.shape
    sets = 2 * windows
    group = xt.shape[2] // windows
    rows = sets * group
    freq = fr.shape[1]
    tiles = freq // LANES
    core, x, y = lax.rem(me, 2), lax.rem(me // 2, 2), me // 4
    upper, side = row // 2, lax.rem(row, 2)
    place = 2 * side + y
    far = (1 - upper, upper)
    column = [4 * far[s] + lax.rem(me, 4) for s in range(STAGES)]

    def flip(bit, by):
        return bit + by * (1 - 2 * bit)

    def masked(mask):
        dx, dy, z = mask >> 1 & 1, mask >> 2 & 1, mask >> 3
        chan = 4 * flip(y, dy) + 2 * flip(x, dx) + flip(core, mask & 1)
        return chan, row + z * (1 - 2 * side)

    def slot_of(chan, win):
        return lax.rem(win, 2) * chan_count + chan

    mine = slot_of(me, row)
    loads = [
        pltpu.make_async_copy(rec_hbm.at[w], rec.at[w], rec_sem.at[w]) for w in range(windows)
    ]
    tables = [
        pltpu.make_async_copy(hbm, vmem, tab_sem.at[i])
        for i, (hbm, vmem) in enumerate(
            ((fwd_hbm, fwd), (band_hbm, band), (lag_hbm, lag), (src_hbm, src_ref))
        )
    ]
    for copy in loads:
        copy.start()
    barrier = pltpu.get_barrier_semaphore()
    for mask in range(1, 2 * chan_count):
        chan, win = masked(mask)
        pl.semaphore_signal(
            barrier, inc=1, device_id={"chan": chan, "win": win}, device_id_type=MESH
        )
    for s in range(STAGES):
        for k in range(2):
            pl.semaphore_signal(
                barrier, inc=1, device_id={"chan": column[s], "win": 2 * (1 - upper) + k},
                device_id_type=MESH,
            )

    for copy in tables:
        copy.start()
    for w in range(windows):
        loads[w].wait()
        for h in range(2):
            tile = rec[w, :, h * LANES : (h + 1) * LANES].T
            for i in range(LANES // group):
                slot = i % 4 // 2 * chan_count + i % 2 * 4 + i // 4
                xt[h, slot, w * group : (w + 1) * group] = tile[i * group : (i + 1) * group]

    pl.semaphore_wait(barrier, 2 * chan_count - 1 + 2 * STAGES)

    for s in range(STAGES):
        for mask in (14, 15, 12, 13, 10, 11, 6, 7, 8, 9, 4, 5, 2, 3, 1):
            chan, win = masked(mask)
            pltpu.make_async_remote_copy(
                src_ref=xt.at[far[s], slot_of(chan, win)], dst_ref=recv.at[s, me, side],
                send_sem=sent.at[0], recv_sem=a_recv.at[s],
                device_id={"chan": chan, "win": win}, device_id_type=MESH,
            ).start()
        pltpu.make_async_copy(xt.at[far[s], mine], recv.at[s, me, side], a_recv.at[s]).start()
    near_row = lax.broadcasted_iota(jnp.int32, (3 * time, time), 0) - time
    near_col = lax.broadcasted_iota(jnp.int32, (3 * time, time), 1)
    near = (jnp.abs(near_row - near_col) <= half_width).astype(F32).astype(BF16)
    root = math.sqrt(0.5)

    def settle(ref, sem):
        pltpu.make_async_copy(ref, ref, sem).wait()

    def normalise(s):
        for i in range(8):
            level = jnp.zeros((rows, time), F32)
            for j in range(max(i - 1, 0), min(i + 1, 7) + 1):
                both = stacked(jnp.abs(recv[s, j].reshape(rows, time)))
                level = level + folded(dot(both, near[(j - i + 1) * time : (j - i + 2) * time]))
            level = level * (1.0 / (2 * half_width + 1))
            nrm[i] = recv[s, i].reshape(rows, time) / jnp.maximum(level, AMPLITUDE_FLOOR)

    def butterfly(block, _):
        at = pl.ds(pl.multiple_of(block * 16, 16), 16)
        low_at = pl.ds(pl.multiple_of(rows + block * 16, 16), 16)
        n = [nrm[i, at, :] for i in range(8)]
        a = [n[i] + n[i + 4] for i in range(4)]
        b = [n[i] - n[i + 4] for i in range(4)]
        even, odd = a[0] + a[2], a[1] + a[3]
        diff, total = root * (b[1] - b[3]), root * (b[1] + b[3])
        pairs = (
            (even + odd, even - odd),
            (b[0] + diff, -(b[2] + total)),
            (a[0] - a[2], a[3] - a[1]),
            (b[0] - diff, b[2] - total),
        )
        for g, pair in enumerate(pairs):
            for k, value in enumerate(pair):
                high, low = halves(value)
                yy[g, at, k * time : (k + 1) * time] = high
                yy[g, low_at, k * time : (k + 1) * time] = low
        return 0

    def transform(s):
        for block in range(rows // 16):
            butterfly(block, 0)
        if s == 0:
            tables[0].wait()
        for g in range(4):
            at = slice(g * LANES, (g + 1) * LANES)
            both = folded(dot(yy[g], fwd[0, g])) + dot(yy[g, :rows], fwd[1, g])
            real, imag = both[:, :LANES], both[:, LANES:]
            fr[:, at] = real
            fi[:, at] = imag
            mm[:, at] = stacked(jnp.sqrt(real * real + imag * imag))

    def whiten(s):
        if s == 0:
            tables[1].wait()
        for g in range(freq // 256):
            at = slice(g * 256, (g + 1) * 256)
            smoothed = folded(dot(mm[...], band[:, at])) / (2 * smooth_reach + 1) + WHITE_EPSILON
            inverse = 1.0 / smoothed
            ww[s, 0, :, at] = fr[:, at] * inverse
            ww[s, 1, :, at] = fi[:, at] * inverse

    def pick(s):
        if s == 0:
            tables[3].wait()
        owned = lax.rem(src_ref[4 * column[s] + place], group)
        for w in range(sets):
            for k in range(2):
                line = 2 * w + k
                gs[s, mine, line : line + 1, :] = ww[s, k, pl.ds(w * group + owned, 1), :]

    def offer(s, mask):
        chan, win = masked(mask)
        return pltpu.make_async_remote_copy(
            src_ref=gs.at[s, mine], dst_ref=gs.at[s, mine],
            send_sem=sent.at[1], recv_sem=g_recv.at[s, mask // 2],
            device_id={"chan": chan, "win": win}, device_id_type=MESH,
        )

    def offers(s, masks):
        for mask in masks:
            offer(s, mask).start()

    def arrive(s, masks):
        for mask in masks:
            offer(s, mask).wait_recv()

    def share(s):
        chan, win = masked(1)
        return pltpu.make_async_remote_copy(
            src_ref=ww.at[s], dst_ref=wo.at[s],
            send_sem=sent.at[2], recv_sem=w_recv.at[0],
            device_id={"chan": chan, "win": win}, device_id_type=MESH,
        )

    for s in range(STAGES):
        settle(recv.at[s], a_recv.at[s])
        if s == 1:
            offers(0, (6, 12, 10, 14))
        normalise(s)
        transform(s)
        whiten(s)
        share(s).start()
        pick(s)
        offers(s, ((1, 2, 4, 8), (2, 4, 8))[s])
    tables[2].wait()

    def compute(sources, entries):
        half = len(entries) * group
        targets = sorted({target for _, target in entries})
        for t in range(tiles):
            at = slice(t * LANES, (t + 1) * LANES)
            sums = {}
            for w in range(sets):
                rows_at = slice(w * group, (w + 1) * group)
                white = {
                    (j, v): tuple((ww, wo)[j][v, k, rows_at, at] for k in range(2))
                    for j, v in targets
                }
                lines = [
                    (gs[s, slot, 2 * w : 2 * w + 1, at], gs[s, slot, 2 * w + 1 : 2 * w + 2, at])
                    for s, slot in sources
                ]
                for n, (source, target) in enumerate(entries):
                    (sr, si), (real, imag) = lines[source], white[target]
                    new = (sr * real + si * imag, sr * imag - si * real)
                    for k in range(2):
                        sums[n, k] = new[k] if w == 0 else sums[n, k] + new[k]
            for n in range(0, len(entries), 2):
                for k in range(2):
                    high, low = halves(jnp.concatenate([sums[n, k], sums[n + 1, k]], axis=0))
                    col = k * freq + t * LANES
                    cc[n * group : (n + 2) * group, col : col + LANES] = high
                    cc[half + n * group : half + (n + 2) * group, col : col + LANES] = low
        return folded(dot(cc[: 2 * half], lag[0])) + dot(cc[:half], lag[1])

    def deliver(staged, landed, j, v, owner, value):
        def send():
            staged[...] = value
            pltpu.make_async_remote_copy(
                src_ref=staged, dst_ref=landed, send_sem=sent.at[3], recv_sem=r_recv.at[0],
                device_id={"win": owner, "chan": column[v] + j * (1 - 2 * core)},
                device_id_type=MESH,
            ).start()

        if j == 1:
            send()
            return
        here = (owner == row) & (column[v] == me)

        @pl.when(here)
        def _():
            landed[...] = value

        @pl.when(jnp.logical_not(here))
        def _():
            send()

    steps = 2 * win_count - 1
    base = side * chan_count + 4 * y + 2 * x
    arrive(0, (1,))
    entries = [(k, (0, v)) for v in range(STAGES) for k in range(2)]
    result = compute([(0, base), (0, base + 1)], entries)
    for n, (k, (_, v)) in enumerate(entries):
        at = slice(n * group, (n + 1) * group)
        spot = pl.ds(pl.multiple_of(y * group, group), group)
        deliver(
            part.at[2 * steps, at], land.at[upper, place, side, k, spot], 0, v,
            2 * far[0] + x, result[at],
        )
    offers(1, (6,))
    settle(wo, w_recv.at[0])
    arrive(0, (4,))
    entries = [(0, (j, v)) for j in range(2) for v in range(STAGES)]
    result = compute([(0, side * chan_count + 4 * (1 - y) + 2 * x + core)], entries)
    for n, (_, (j, v)) in enumerate(entries):
        at = slice(n * group, (n + 1) * group)
        spot = pl.ds(pl.multiple_of((1 - y) * group, group), group)
        deliver(
            part.at[2 * steps + 2, at], land.at[upper, place, side, core, spot], j, v,
            2 * far[0] + x, result[at],
        )

    def forward():
        arrive(1, (8,))
        for target in (2, 4, 6):
            chan, win = masked(target)
            slot = gs.at[1, slot_of(*masked(8))]
            pltpu.make_async_remote_copy(
                src_ref=slot, dst_ref=slot, send_sem=sent.at[1], recv_sem=g_recv.at[1, 4 + target // 2],
                device_id={"chan": chan, "win": win}, device_id_type=MESH,
            ).start()

    def step(q, _):
        s = (q + 1) // 4
        i = q - 3 * s
        e = flip(x, 1 - upper)
        early = (2 - i) * (1 - i) // 2 * (2 - e) + i * (2 - i) * (1 + 2 * e) + i * (i - 1) // 2 * (3 - e)
        t = (1 - s) * early + s * (2 * lax.rem(i, 2) + flip(i // 2, flip(x, upper)))
        at_x, r = flip(x, lax.rem(t, 2)), flip(side, t // 2)
        owner = 2 * (far[0] + s * (far[1] - far[0])) + at_x
        @pl.when(q == 1)
        def _():
            forward()

        for k, masks in enumerate(((4,), (2, 6), (8, 12), (10, 14))):
            for stage in range(1 - min(k, 1), STAGES):
                @pl.when((s == stage) & (t == k))
                def _():
                    arrive(stage, masks[stage:] if k == 2 else masks)

        slots = [(s, r * chan_count + 4 * there + 2 * at_x + core) for there in range(2)]
        entries = [(n, (j, v)) for j in range(2) for v in range(STAGES) for n in range(2)]
        result = compute(slots, entries)
        for j in (1, 0):
            for v in range(STAGES):
                first = (2 * j + v) * 2 * group
                deliver(
                    part.at[2 * q + j, v * 2 * group : (v + 1) * 2 * group],
                    land.at[upper, place, r, core], j, v, owner, result[first : first + 2 * group],
                )
        return 0

    lax.fori_loop(0, steps, step, 0)

    settle(part.at[: 2 * steps + 1], r_recv.at[0])
    for g in range(4):
        for r in range(2):
            for k in range(2):
                for there in range(2):
                    at = slice(there * group, (there + 1) * group)
                    to = ((4 * k + 2 * r + there) * 4 + g) * group
                    out_ref[to : to + group, :] = land[0, g, r, k, at] + land[1, g, r, k, at]

    settle(part.at[: 2 * steps + 1], sent.at[0])
    settle(gs.at[0, : 2 * chan_count - 1], sent.at[1])
    settle(ww, sent.at[2])
    settle(part.at[: 2 * steps + 1], sent.at[3])


def fused(records, sources):
    chan_count, win_count = lax.axis_size("chan"), lax.axis_size("win")
    windows, time, channels = records.shape
    length = time * chan_count
    freq = length // 2
    group = channels // chan_count // 4
    sets = 2 * windows
    rows = sets * group
    source_count = sources.shape[0]
    lag_count = length // 4
    reach = length // 32
    half_width = min(16, time)
    owned = source_count // win_count
    factor = 1.0 / math.sqrt(windows * win_count * freq)
    fwd = forward_blocks(length, time)
    band = smooth_table(freq, reach)
    lag = lag_table(length, lag_count, factor)
    width = STAGES * group
    block = owned * 2 * width
    vmem = pl.BlockSpec(memory_space=pltpu.VMEM)
    hbm = pl.BlockSpec(memory_space=pltpu.HBM)
    dma = pltpu.SemaphoreType.DMA
    out = pl.pallas_call(
        functools.partial(fused_kernel, half_width, reach, chan_count, win_count),
        out_shape=pltpu.VMEM((block, lag_count), F32),
        in_specs=[hbm] * 5,
        out_specs=vmem,
        scratch_shapes=[
            pltpu.SMEM(sources.shape, jnp.int32),
            pltpu.VMEM(records.shape, F32),
            pltpu.VMEM((2, 2 * chan_count, windows * group, time), F32),
            pltpu.VMEM((STAGES, chan_count, 2, windows * group, time), F32),
            pltpu.VMEM((chan_count, rows, time), F32),
            pltpu.VMEM((4, 2 * rows, 2 * time), BF16),
            pltpu.VMEM((rows, freq), F32),
            pltpu.VMEM((rows, freq), F32),
            pltpu.VMEM((2 * rows, freq), BF16),
            pltpu.VMEM((STAGES, 2, rows, freq), F32),
            pltpu.VMEM((STAGES, 2, rows, freq), F32),
            pltpu.VMEM((STAGES, 2 * chan_count, 2 * sets, freq), F32),
            pltpu.VMEM((16 * group, 2 * freq), BF16),
            pltpu.VMEM((4 * win_count + 2, 4 * group, lag_count), F32),
            pltpu.VMEM((2, 4, 2, 2, 2 * group, lag_count), F32),
            pltpu.VMEM(fwd.shape, BF16),
            pltpu.VMEM(band.shape, BF16),
            pltpu.VMEM(lag.shape, BF16),
            dma((windows,)),
            dma((4,)),
            dma((4,)),
            dma((STAGES,)),
            dma((STAGES, chan_count)),
            dma((1,)),
            dma((1,)),
        ],
        compiler_params=pltpu.CompilerParams(
            collective_id=0, has_side_effects=True, vmem_limit_bytes=40_000_000
        ),
        name="interferometry",
    )(*[
        pltpu.with_memory_space_constraint(value, pltpu.HBM)
        for value in (sources, records, jnp.asarray(fwd), jnp.asarray(band), jnp.asarray(lag))
    ])
    return out.reshape(owned, 2 * width, lag_count).transpose(0, 2, 1)


def fits(records, sources):
    chan_count, win_count = lax.axis_size("chan"), lax.axis_size("win")
    windows, time, channels = records.shape
    return (
        time == LANES and chan_count == 8 and win_count == 4 and channels % LANES == 0
        and channels == 32 * chan_count and sources.shape[0] == 4 * chan_count
        and windows % 2 == 0
    )


def body(records, sources):
    return fused(records, sources) if fits(records, sources) else local(records, sources)


def solution(mesh):
    placed = (P("win", "chan", None), P())
    return jax.shard_map(
        body, mesh=mesh, in_specs=placed, out_specs=P("win", None, "chan"), check_vma=False
    )
```

```python
import functools
import math

import jax
import jax.numpy as jnp
import numpy as np
from jax import lax
from jax.experimental import pallas as pl
from jax.experimental.pallas import tpu as pltpu
from jax.sharding import PartitionSpec as P

HIGHEST = lax.Precision.HIGHEST
AMPLITUDE_FLOOR = 0.25
WHITE_EPSILON = 1e-06


def fourier_table(length):
    freq_count = length // 2
    freqs = jnp.arange(freq_count, dtype=jnp.int32)[:, None]
    sample_index = jnp.arange(length, dtype=jnp.int32)[None, :]
    angles = (freqs * sample_index % length).astype(jnp.float32) * (2.0 * math.pi / length)
    return jnp.concatenate([jnp.cos(angles), -jnp.sin(angles)], axis=0)


def band_table(freq_count, reach):
    rows_index = jnp.arange(freq_count, dtype=jnp.int32)[:, None]
    cols_index = jnp.arange(freq_count, dtype=jnp.int32)[None, :]
    return (jnp.abs(rows_index - cols_index) <= reach).astype(jnp.float32)


def inverse_table(length, lag_count, first_bin, bin_count, factor):
    freqs = first_bin + jnp.arange(bin_count, dtype=jnp.int32)
    lag_index = jnp.arange(lag_count, dtype=jnp.int32) - lag_count // 2
    angles = (lag_index[:, None] * freqs[None, :] % length).astype(jnp.float32) * (
        2.0 * math.pi / length
    )
    weights = jnp.where(freqs == 0, 1.0, 2.0).astype(jnp.float32)[None, :] * factor
    return jnp.concatenate([weights * jnp.cos(angles), -weights * jnp.sin(angles)], axis=1)


def running_level(padded, time_count, window_span):
    window_total = padded.shape[0]
    chans = padded.shape[2]
    running = jnp.concatenate(
        [jnp.zeros((window_total, 1, chans), jnp.float32), jnp.cumsum(jnp.abs(padded), axis=1)],
        axis=1,
    )
    return (running[:, window_span:] - running[:, :time_count]) / window_span


def local(records, sources):
    chan_count = lax.axis_size("chan")
    local_windows, local_time, all_channels = records.shape
    length = local_time * chan_count
    freq_count = length // 2
    chan_width = all_channels // chan_count
    half_width = min(16, local_time)
    smooth_reach = length // 32
    window_span = 2 * half_width + 1
    lag_count = length // 4
    forward = fourier_table(length)
    band_matrix = band_table(freq_count, smooth_reach)
    pieces = lax.all_to_all(records, "chan", split_axis=2, concat_axis=1, tiled=True)
    padded = jnp.pad(pieces, ((0, 0), (half_width, half_width), (0, 0)))
    amplitude = running_level(padded, length, window_span)
    whiten_pieces = pieces / jnp.maximum(amplitude, AMPLITUDE_FLOOR)
    spectrum = jnp.einsum("kt,wtc->wkc", forward, whiten_pieces, precision=HIGHEST)
    real_part = spectrum[:, :freq_count]
    imag_part = spectrum[:, freq_count:]
    magnitude = jnp.sqrt(real_part * real_part + imag_part * imag_part)
    smoothed = (
        jnp.einsum("jk,wkc->wjc", band_matrix, magnitude, precision=HIGHEST)
        / (2 * smooth_reach + 1)
        + WHITE_EPSILON
    )
    whitened = jnp.stack([real_part / smoothed, imag_part / smoothed], axis=1)
    band_data = lax.all_to_all(whitened, "win", split_axis=2, concat_axis=0, tiled=True)
    total_windows = band_data.shape[0]
    band_count = band_data.shape[2]
    source_count = sources.shape[0]
    chan_index = lax.axis_index("chan")
    channel_ids = jnp.arange(chan_width, dtype=jnp.int32)
    per_device = source_count // chan_count
    owned_local = (
        lax.dynamic_slice_in_dim(sources, chan_index * per_device, per_device)
        - chan_index * chan_width
    )
    selector = (owned_local[:, None] == channel_ids[None, :]).astype(jnp.float32)
    chosen = jnp.einsum("sc,wafc->wafs", selector, band_data, precision=HIGHEST)
    spectra = lax.all_gather(chosen, "chan", axis=3, tiled=True)
    source_real = spectra[:, 0]
    source_imag = spectra[:, 1]
    white_real = band_data[:, 0]
    white_imag = band_data[:, 1]
    cross_real = jnp.einsum(
        "wfs,wfc->fsc", source_real, white_real, precision=HIGHEST
    ) + jnp.einsum("wfs,wfc->fsc", source_imag, white_imag, precision=HIGHEST)
    cross_imag = jnp.einsum(
        "wfs,wfc->fsc", source_real, white_imag, precision=HIGHEST
    ) - jnp.einsum("wfs,wfc->fsc", source_imag, white_real, precision=HIGHEST)
    stacked = jnp.stack([cross_real, cross_imag])
    factor = 1.0 / math.sqrt(total_windows * freq_count)
    band_start = lax.axis_index("win") * band_count
    band_table_part = inverse_table(length, lag_count, band_start, band_count, factor).reshape(
        lag_count, 2, band_count
    )
    return lax.psum_scatter(
        jnp.einsum("tak,aksc->stc", band_table_part, stacked, precision=HIGHEST),
        "win",
        scatter_dimension=0,
        tiled=True,
    )


LANES = 128
STAGES = 2
BF16 = jnp.bfloat16
F32 = jnp.float32
MESH = pl.DeviceIdType.MESH


def bin_order(freq_count):
    per = freq_count // 8
    pairs = ((0, 4), (1, 7), (2, 6), (3, 5))
    return np.concatenate([8 * np.arange(per) + m for pair in pairs for m in pair])


def split_table(table):
    high = table.astype(np.float32).astype(BF16)
    low = (table - high.astype(np.float64)).astype(np.float32).astype(BF16)
    return np.stack([high, low])


def forward_blocks(length, time):
    per = length // 16
    rows = np.arange(time)[:, None]
    blocks = []
    for first, second in ((0, 4), (1, 7), (2, 6), (3, 5)):
        angle1 = 2 * np.pi * ((8 * np.arange(per) + first)[None, :] * rows % length) / length
        angle2 = 2 * np.pi * ((8 * np.arange(per) + second)[None, :] * rows % length) / length
        c1, s1, c2, s2 = np.cos(angle1), np.sin(angle1), np.cos(angle2), np.sin(angle2)
        if first == 0:
            zero = np.zeros_like(c1)
            top = np.concatenate([c1, zero, -s1, zero], axis=1)
            low = np.concatenate([zero, c2, zero, -s2], axis=1)
        else:
            top = np.concatenate([c1, c2, -s1, -s2], axis=1)
            low = np.concatenate([s1, -s2, c1, -c2], axis=1)
        blocks.append(np.concatenate([top, low], axis=0))
    return split_table(np.stack(blocks))


def smooth_table(freq_count, reach):
    order = bin_order(freq_count)
    return (np.abs(order[:, None] - order[None, :]) <= reach).astype(np.float32).astype(BF16)


def lag_table(length, lag_count, factor):
    bins = bin_order(length // 2)[:, None]
    lags = (np.arange(lag_count) - lag_count // 2)[None, :]
    angle = 2 * np.pi * (bins * lags % length) / length
    weight = np.where(bins == 0, 1.0, 2.0) * factor
    return split_table(np.concatenate([weight * np.cos(angle), -weight * np.sin(angle)], axis=0))


def halves(value):
    high = value.astype(BF16)
    return high, (value - high.astype(F32)).astype(BF16)


def stacked(value):
    return jnp.concatenate(halves(value), axis=0)


def dot(a, b):
    return jnp.dot(a, b, preferred_element_type=F32)


def folded(product):
    half = product.shape[0] // 2
    return product[:half] + product[half:]


def fused_kernel(
    half_width, smooth_reach, chan_count, win_count,
    src_hbm, rec_hbm, fwd_hbm, band_hbm, lag_hbm, out_ref,
    src_ref, rec, xt, recv, nrm, yy, fr, fi, mm, ww, wo, gs, cc, part, land,
    fwd, band, lag,
    rec_sem, tab_sem, sent, a_recv, g_recv, w_recv, r_recv,
):
    me = lax.axis_index("chan")
    row = lax.axis_index("win")
    windows, time, _ = rec.shape
    sets = 2 * windows
    group = xt.shape[2] // windows
    rows = sets * group
    freq = fr.shape[1]
    tiles = freq // LANES
    core, x, y = lax.rem(me, 2), lax.rem(me // 2, 2), me // 4
    upper, side = row // 2, lax.rem(row, 2)
    place = 2 * side + y
    far = (1 - upper, upper)
    column = [4 * far[s] + lax.rem(me, 4) for s in range(STAGES)]

    def flip(bit, by):
        return bit + by * (1 - 2 * bit)

    def masked(mask):
        dx, dy, z = mask >> 1 & 1, mask >> 2 & 1, mask >> 3
        chan = 4 * flip(y, dy) + 2 * flip(x, dx) + flip(core, mask & 1)
        return chan, row + z * (1 - 2 * side)

    def slot_of(chan, win):
        return lax.rem(win, 2) * chan_count + chan

    mine = slot_of(me, row)
    loads = [
        pltpu.make_async_copy(rec_hbm.at[w], rec.at[w], rec_sem.at[w]) for w in range(windows)
    ]
    tables = [
        pltpu.make_async_copy(hbm, vmem, tab_sem.at[i])
        for i, (hbm, vmem) in enumerate(
            ((fwd_hbm, fwd), (band_hbm, band), (lag_hbm, lag), (src_hbm, src_ref))
        )
    ]
    for copy in loads:
        copy.start()
    barrier = pltpu.get_barrier_semaphore()
    for mask in range(1, 2 * chan_count):
        chan, win = masked(mask)
        pl.semaphore_signal(
            barrier, inc=1, device_id={"chan": chan, "win": win}, device_id_type=MESH
        )
    for s in range(STAGES):
        for k in range(2):
            pl.semaphore_signal(
                barrier, inc=1, device_id={"chan": column[s], "win": 2 * (1 - upper) + k},
                device_id_type=MESH,
            )

    for copy in tables:
        copy.start()
    for w in range(windows):
        loads[w].wait()
        for h in range(2):
            tile = rec[w, :, h * LANES : (h + 1) * LANES].T
            for i in range(LANES // group):
                slot = i % 4 // 2 * chan_count + i % 2 * 4 + i // 4
                xt[h, slot, w * group : (w + 1) * group] = tile[i * group : (i + 1) * group]

    pl.semaphore_wait(barrier, 2 * chan_count - 1 + 2 * STAGES)

    for s in range(STAGES):
        for mask in (14, 15, 12, 13, 10, 11, 6, 7, 8, 9, 4, 5, 2, 3, 1):
            chan, win = masked(mask)
            pltpu.make_async_remote_copy(
                src_ref=xt.at[far[s], slot_of(chan, win)], dst_ref=recv.at[s, me, side],
                send_sem=sent.at[0], recv_sem=a_recv.at[s],
                device_id={"chan": chan, "win": win}, device_id_type=MESH,
            ).start()
        pltpu.make_async_copy(xt.at[far[s], mine], recv.at[s, me, side], a_recv.at[s]).start()
    near_row = lax.broadcasted_iota(jnp.int32, (3 * time, time), 0) - time
    near_col = lax.broadcasted_iota(jnp.int32, (3 * time, time), 1)
    near = (jnp.abs(near_row - near_col) <= half_width).astype(F32).astype(BF16)
    root = math.sqrt(0.5)

    def settle(ref, sem):
        pltpu.make_async_copy(ref, ref, sem).wait()

    def normalise(s):
        for i in range(8):
            level = jnp.zeros((rows, time), F32)
            for j in range(max(i - 1, 0), min(i + 1, 7) + 1):
                both = stacked(jnp.abs(recv[s, j].reshape(rows, time)))
                level = level + folded(dot(both, near[(j - i + 1) * time : (j - i + 2) * time]))
            level = level * (1.0 / (2 * half_width + 1))
            nrm[i] = recv[s, i].reshape(rows, time) / jnp.maximum(level, AMPLITUDE_FLOOR)

    def butterfly(block, _):
        at = pl.ds(pl.multiple_of(block * 16, 16), 16)
        low_at = pl.ds(pl.multiple_of(rows + block * 16, 16), 16)
        n = [nrm[i, at, :] for i in range(8)]
        a = [n[i] + n[i + 4] for i in range(4)]
        b = [n[i] - n[i + 4] for i in range(4)]
        even, odd = a[0] + a[2], a[1] + a[3]
        diff, total = root * (b[1] - b[3]), root * (b[1] + b[3])
        pairs = (
            (even + odd, even - odd),
            (b[0] + diff, -(b[2] + total)),
            (a[0] - a[2], a[3] - a[1]),
            (b[0] - diff, b[2] - total),
        )
        for g, pair in enumerate(pairs):
            for k, value in enumerate(pair):
                high, low = halves(value)
                yy[g, at, k * time : (k + 1) * time] = high
                yy[g, low_at, k * time : (k + 1) * time] = low
        return 0

    def transform(s):
        for block in range(rows // 16):
            butterfly(block, 0)
        if s == 0:
            tables[0].wait()
        for g in range(4):
            at = slice(g * LANES, (g + 1) * LANES)
            both = folded(dot(yy[g], fwd[0, g])) + dot(yy[g, :rows], fwd[1, g])
            real, imag = both[:, :LANES], both[:, LANES:]
            fr[:, at] = real
            fi[:, at] = imag
            mm[:, at] = stacked(jnp.sqrt(real * real + imag * imag))

    def whiten(s):
        if s == 0:
            tables[1].wait()
        for g in range(freq // 256):
            at = slice(g * 256, (g + 1) * 256)
            smoothed = folded(dot(mm[...], band[:, at])) / (2 * smooth_reach + 1) + WHITE_EPSILON
            inverse = 1.0 / smoothed
            ww[s, 0, :, at] = fr[:, at] * inverse
            ww[s, 1, :, at] = fi[:, at] * inverse

    def pick(s):
        if s == 0:
            tables[3].wait()
        owned = lax.rem(src_ref[4 * column[s] + place], group)
        for w in range(sets):
            for k in range(2):
                line = 2 * w + k
                gs[s, mine, line : line + 1, :] = ww[s, k, pl.ds(w * group + owned, 1), :]

    def offer(s, mask):
        chan, win = masked(mask)
        return pltpu.make_async_remote_copy(
            src_ref=gs.at[s, mine], dst_ref=gs.at[s, mine],
            send_sem=sent.at[1], recv_sem=g_recv.at[s, mask // 2],
            device_id={"chan": chan, "win": win}, device_id_type=MESH,
        )

    def offers(s, masks):
        for mask in masks:
            offer(s, mask).start()

    def arrive(s, masks):
        for mask in masks:
            offer(s, mask).wait_recv()

    def share(s):
        chan, win = masked(1)
        return pltpu.make_async_remote_copy(
            src_ref=ww.at[s], dst_ref=wo.at[s],
            send_sem=sent.at[2], recv_sem=w_recv.at[0],
            device_id={"chan": chan, "win": win}, device_id_type=MESH,
        )

    for s in range(STAGES):
        settle(recv.at[s], a_recv.at[s])
        if s == 1:
            offers(0, (6, 12, 10, 14))
        normalise(s)
        transform(s)
        whiten(s)
        share(s).start()
        pick(s)
        offers(s, ((1, 2, 4, 8), (8,))[s])
    tables[2].wait()

    def compute(sources, entries):
        half = len(entries) * group
        targets = sorted({target for _, target in entries})
        for t in range(tiles):
            at = slice(t * LANES, (t + 1) * LANES)
            sums = {}
            for w in range(sets):
                rows_at = slice(w * group, (w + 1) * group)
                white = {
                    (j, v): tuple((ww, wo)[j][v, k, rows_at, at] for k in range(2))
                    for j, v in targets
                }
                lines = [
                    (gs[s, slot, 2 * w : 2 * w + 1, at], gs[s, slot, 2 * w + 1 : 2 * w + 2, at])
                    for s, slot in sources
                ]
                for n, (source, target) in enumerate(entries):
                    (sr, si), (real, imag) = lines[source], white[target]
                    new = (sr * real + si * imag, sr * imag - si * real)
                    for k in range(2):
                        sums[n, k] = new[k] if w == 0 else sums[n, k] + new[k]
            for n in range(0, len(entries), 2):
                for k in range(2):
                    high, low = halves(jnp.concatenate([sums[n, k], sums[n + 1, k]], axis=0))
                    col = k * freq + t * LANES
                    cc[n * group : (n + 2) * group, col : col + LANES] = high
                    cc[half + n * group : half + (n + 2) * group, col : col + LANES] = low
        return folded(dot(cc[: 2 * half], lag[0])) + dot(cc[:half], lag[1])

    def deliver(staged, landed, j, v, owner, value):
        def send():
            staged[...] = value
            pltpu.make_async_remote_copy(
                src_ref=staged, dst_ref=landed, send_sem=sent.at[3], recv_sem=r_recv.at[0],
                device_id={"win": owner, "chan": column[v] + j * (1 - 2 * core)},
                device_id_type=MESH,
            ).start()

        if j == 1:
            send()
            return
        here = (owner == row) & (column[v] == me)

        @pl.when(here)
        def _():
            landed[...] = value

        @pl.when(jnp.logical_not(here))
        def _():
            send()

    steps = 2 * win_count - 1
    base = side * chan_count + 4 * y + 2 * x
    arrive(0, (1,))
    entries = [(k, (0, v)) for v in range(STAGES) for k in range(2)]
    result = compute([(0, base), (0, base + 1)], entries)
    for n, (k, (_, v)) in enumerate(entries):
        at = slice(n * group, (n + 1) * group)
        spot = pl.ds(pl.multiple_of(y * group, group), group)
        deliver(
            part.at[2 * steps, at], land.at[upper, place, side, k, spot], 0, v,
            2 * far[0] + x, result[at],
        )
    offers(1, (2, 4, 6))
    settle(wo, w_recv.at[0])
    arrive(0, (4,))
    entries = [(0, (j, v)) for j in range(2) for v in range(STAGES)]
    result = compute([(0, side * chan_count + 4 * (1 - y) + 2 * x + core)], entries)
    for n, (_, (j, v)) in enumerate(entries):
        at = slice(n * group, (n + 1) * group)
        spot = pl.ds(pl.multiple_of((1 - y) * group, group), group)
        deliver(
            part.at[2 * steps + 2, at], land.at[upper, place, side, core, spot], j, v,
            2 * far[0] + x, result[at],
        )

    def forward():
        arrive(1, (8,))
        for target in (2, 4, 6):
            chan, win = masked(target)
            slot = gs.at[1, slot_of(*masked(8))]
            pltpu.make_async_remote_copy(
                src_ref=slot, dst_ref=slot, send_sem=sent.at[1], recv_sem=g_recv.at[1, 4 + target // 2],
                device_id={"chan": chan, "win": win}, device_id_type=MESH,
            ).start()

    def step(q, _):
        s = (q + 1) // 4
        i = q - 3 * s
        e = flip(x, 1 - upper)
        early = (2 - i) * (1 - i) // 2 * (2 - e) + i * (2 - i) * (1 + 2 * e) + i * (i - 1) // 2 * (3 - e)
        t = (1 - s) * early + s * ((side + upper - 2 * side * upper) * (2 * lax.rem(i, 2) + flip(i // 2, flip(x, upper))) + (1 - (side + upper - 2 * side * upper)) * (2 * (i // 2) + flip(lax.rem(i, 2), flip(x, upper))))
        at_x, r = flip(x, lax.rem(t, 2)), flip(side, t // 2)
        owner = 2 * (far[0] + s * (far[1] - far[0])) + at_x
        @pl.when(q == 1)
        def _():
            forward()

        for k, masks in enumerate(((4,), (2, 6), (8, 12), (10, 14))):
            for stage in range(1 - min(k, 1), STAGES):
                @pl.when((s == stage) & (t == k))
                def _():
                    arrive(stage, masks[stage:] if k == 2 else masks)

        slots = [(s, r * chan_count + 4 * there + 2 * at_x + core) for there in range(2)]
        entries = [(n, (j, v)) for j in range(2) for v in range(STAGES) for n in range(2)]
        result = compute(slots, entries)
        for j in (1, 0):
            for v in range(STAGES):
                first = (2 * j + v) * 2 * group
                deliver(
                    part.at[2 * q + j, v * 2 * group : (v + 1) * 2 * group],
                    land.at[upper, place, r, core], j, v, owner, result[first : first + 2 * group],
                )
        return 0

    lax.fori_loop(0, steps, step, 0)

    settle(part.at[: 2 * steps + 1], r_recv.at[0])
    for g in range(4):
        for r in range(2):
            for k in range(2):
                for there in range(2):
                    at = slice(there * group, (there + 1) * group)
                    to = ((4 * k + 2 * r + there) * 4 + g) * group
                    out_ref[to : to + group, :] = land[0, g, r, k, at] + land[1, g, r, k, at]

    settle(part.at[: 2 * steps + 1], sent.at[0])
    settle(gs.at[0, : 2 * chan_count - 1], sent.at[1])
    settle(ww, sent.at[2])
    settle(part.at[: 2 * steps + 1], sent.at[3])


def fused(records, sources):
    chan_count, win_count = lax.axis_size("chan"), lax.axis_size("win")
    windows, time, channels = records.shape
    length = time * chan_count
    freq = length // 2
    group = channels // chan_count // 4
    sets = 2 * windows
    rows = sets * group
    source_count = sources.shape[0]
    lag_count = length // 4
    reach = length // 32
    half_width = min(16, time)
    owned = source_count // win_count
    factor = 1.0 / math.sqrt(windows * win_count * freq)
    fwd = forward_blocks(length, time)
    band = smooth_table(freq, reach)
    lag = lag_table(length, lag_count, factor)
    width = STAGES * group
    block = owned * 2 * width
    vmem = pl.BlockSpec(memory_space=pltpu.VMEM)
    hbm = pl.BlockSpec(memory_space=pltpu.HBM)
    dma = pltpu.SemaphoreType.DMA
    out = pl.pallas_call(
        functools.partial(fused_kernel, half_width, reach, chan_count, win_count),
        out_shape=pltpu.VMEM((block, lag_count), F32),
        in_specs=[hbm] * 5,
        out_specs=vmem,
        scratch_shapes=[
            pltpu.SMEM(sources.shape, jnp.int32),
            pltpu.VMEM(records.shape, F32),
            pltpu.VMEM((2, 2 * chan_count, windows * group, time), F32),
            pltpu.VMEM((STAGES, chan_count, 2, windows * group, time), F32),
            pltpu.VMEM((chan_count, rows, time), F32),
            pltpu.VMEM((4, 2 * rows, 2 * time), BF16),
            pltpu.VMEM((rows, freq), F32),
            pltpu.VMEM((rows, freq), F32),
            pltpu.VMEM((2 * rows, freq), BF16),
            pltpu.VMEM((STAGES, 2, rows, freq), F32),
            pltpu.VMEM((STAGES, 2, rows, freq), F32),
            pltpu.VMEM((STAGES, 2 * chan_count, 2 * sets, freq), F32),
            pltpu.VMEM((16 * group, 2 * freq), BF16),
            pltpu.VMEM((4 * win_count + 2, 4 * group, lag_count), F32),
            pltpu.VMEM((2, 4, 2, 2, 2 * group, lag_count), F32),
            pltpu.VMEM(fwd.shape, BF16),
            pltpu.VMEM(band.shape, BF16),
            pltpu.VMEM(lag.shape, BF16),
            dma((windows,)),
            dma((4,)),
            dma((4,)),
            dma((STAGES,)),
            dma((STAGES, chan_count)),
            dma((1,)),
            dma((1,)),
        ],
        compiler_params=pltpu.CompilerParams(
            collective_id=0, has_side_effects=True, vmem_limit_bytes=40_000_000
        ),
        name="interferometry",
    )(*[
        pltpu.with_memory_space_constraint(value, pltpu.HBM)
        for value in (sources, records, jnp.asarray(fwd), jnp.asarray(band), jnp.asarray(lag))
    ])
    return out.reshape(owned, 2 * width, lag_count).transpose(0, 2, 1)


def fits(records, sources):
    chan_count, win_count = lax.axis_size("chan"), lax.axis_size("win")
    windows, time, channels = records.shape
    return (
        time == LANES and chan_count == 8 and win_count == 4 and channels % LANES == 0
        and channels == 32 * chan_count and sources.shape[0] == 4 * chan_count
        and windows % 2 == 0
    )


def body(records, sources):
    return fused(records, sources) if fits(records, sources) else local(records, sources)


def solution(mesh):
    placed = (P("win", "chan", None), P())
    return jax.shard_map(
        body, mesh=mesh, in_specs=placed, out_specs=P("win", None, "chan"), check_vma=False
    )
```

```python
import functools
import math

import jax
import jax.numpy as jnp
import numpy as np
from jax import lax
from jax.experimental import pallas as pl
from jax.experimental.pallas import tpu as pltpu
from jax.sharding import PartitionSpec as P

HIGHEST = lax.Precision.HIGHEST
AMPLITUDE_FLOOR = 0.25
WHITE_EPSILON = 1e-06


def fourier_table(length):
    freq_count = length // 2
    freqs = jnp.arange(freq_count, dtype=jnp.int32)[:, None]
    sample_index = jnp.arange(length, dtype=jnp.int32)[None, :]
    angles = (freqs * sample_index % length).astype(jnp.float32) * (2.0 * math.pi / length)
    return jnp.concatenate([jnp.cos(angles), -jnp.sin(angles)], axis=0)


def band_table(freq_count, reach):
    rows_index = jnp.arange(freq_count, dtype=jnp.int32)[:, None]
    cols_index = jnp.arange(freq_count, dtype=jnp.int32)[None, :]
    return (jnp.abs(rows_index - cols_index) <= reach).astype(jnp.float32)


def inverse_table(length, lag_count, first_bin, bin_count, factor):
    freqs = first_bin + jnp.arange(bin_count, dtype=jnp.int32)
    lag_index = jnp.arange(lag_count, dtype=jnp.int32) - lag_count // 2
    angles = (lag_index[:, None] * freqs[None, :] % length).astype(jnp.float32) * (
        2.0 * math.pi / length
    )
    weights = jnp.where(freqs == 0, 1.0, 2.0).astype(jnp.float32)[None, :] * factor
    return jnp.concatenate([weights * jnp.cos(angles), -weights * jnp.sin(angles)], axis=1)


def running_level(padded, time_count, window_span):
    window_total = padded.shape[0]
    chans = padded.shape[2]
    running = jnp.concatenate(
        [jnp.zeros((window_total, 1, chans), jnp.float32), jnp.cumsum(jnp.abs(padded), axis=1)],
        axis=1,
    )
    return (running[:, window_span:] - running[:, :time_count]) / window_span


def local(records, sources):
    chan_count = lax.axis_size("chan")
    local_windows, local_time, all_channels = records.shape
    length = local_time * chan_count
    freq_count = length // 2
    chan_width = all_channels // chan_count
    half_width = min(16, local_time)
    smooth_reach = length // 32
    window_span = 2 * half_width + 1
    lag_count = length // 4
    forward = fourier_table(length)
    band_matrix = band_table(freq_count, smooth_reach)
    pieces = lax.all_to_all(records, "chan", split_axis=2, concat_axis=1, tiled=True)
    padded = jnp.pad(pieces, ((0, 0), (half_width, half_width), (0, 0)))
    amplitude = running_level(padded, length, window_span)
    whiten_pieces = pieces / jnp.maximum(amplitude, AMPLITUDE_FLOOR)
    spectrum = jnp.einsum("kt,wtc->wkc", forward, whiten_pieces, precision=HIGHEST)
    real_part = spectrum[:, :freq_count]
    imag_part = spectrum[:, freq_count:]
    magnitude = jnp.sqrt(real_part * real_part + imag_part * imag_part)
    smoothed = (
        jnp.einsum("jk,wkc->wjc", band_matrix, magnitude, precision=HIGHEST)
        / (2 * smooth_reach + 1)
        + WHITE_EPSILON
    )
    whitened = jnp.stack([real_part / smoothed, imag_part / smoothed], axis=1)
    band_data = lax.all_to_all(whitened, "win", split_axis=2, concat_axis=0, tiled=True)
    total_windows = band_data.shape[0]
    band_count = band_data.shape[2]
    source_count = sources.shape[0]
    chan_index = lax.axis_index("chan")
    channel_ids = jnp.arange(chan_width, dtype=jnp.int32)
    per_device = source_count // chan_count
    owned_local = (
        lax.dynamic_slice_in_dim(sources, chan_index * per_device, per_device)
        - chan_index * chan_width
    )
    selector = (owned_local[:, None] == channel_ids[None, :]).astype(jnp.float32)
    chosen = jnp.einsum("sc,wafc->wafs", selector, band_data, precision=HIGHEST)
    spectra = lax.all_gather(chosen, "chan", axis=3, tiled=True)
    source_real = spectra[:, 0]
    source_imag = spectra[:, 1]
    white_real = band_data[:, 0]
    white_imag = band_data[:, 1]
    cross_real = jnp.einsum(
        "wfs,wfc->fsc", source_real, white_real, precision=HIGHEST
    ) + jnp.einsum("wfs,wfc->fsc", source_imag, white_imag, precision=HIGHEST)
    cross_imag = jnp.einsum(
        "wfs,wfc->fsc", source_real, white_imag, precision=HIGHEST
    ) - jnp.einsum("wfs,wfc->fsc", source_imag, white_real, precision=HIGHEST)
    stacked = jnp.stack([cross_real, cross_imag])
    factor = 1.0 / math.sqrt(total_windows * freq_count)
    band_start = lax.axis_index("win") * band_count
    band_table_part = inverse_table(length, lag_count, band_start, band_count, factor).reshape(
        lag_count, 2, band_count
    )
    return lax.psum_scatter(
        jnp.einsum("tak,aksc->stc", band_table_part, stacked, precision=HIGHEST),
        "win",
        scatter_dimension=0,
        tiled=True,
    )


LANES = 128
STAGES = 2
BF16 = jnp.bfloat16
F32 = jnp.float32
MESH = pl.DeviceIdType.MESH


def bin_order(freq_count):
    per = freq_count // 8
    pairs = ((0, 4), (1, 7), (2, 6), (3, 5))
    return np.concatenate([8 * np.arange(per) + m for pair in pairs for m in pair])


def split_table(table):
    high = table.astype(np.float32).astype(BF16)
    low = (table - high.astype(np.float64)).astype(np.float32).astype(BF16)
    return np.stack([high, low])


def forward_blocks(length, time):
    per = length // 16
    rows = np.arange(time)[:, None]
    blocks = []
    for first, second in ((0, 4), (1, 7), (2, 6), (3, 5)):
        angle1 = 2 * np.pi * ((8 * np.arange(per) + first)[None, :] * rows % length) / length
        angle2 = 2 * np.pi * ((8 * np.arange(per) + second)[None, :] * rows % length) / length
        c1, s1, c2, s2 = np.cos(angle1), np.sin(angle1), np.cos(angle2), np.sin(angle2)
        if first == 0:
            zero = np.zeros_like(c1)
            top = np.concatenate([c1, zero, -s1, zero], axis=1)
            low = np.concatenate([zero, c2, zero, -s2], axis=1)
        else:
            top = np.concatenate([c1, c2, -s1, -s2], axis=1)
            low = np.concatenate([s1, -s2, c1, -c2], axis=1)
        blocks.append(np.concatenate([top, low], axis=0))
    return split_table(np.stack(blocks))


def smooth_table(freq_count, reach):
    order = bin_order(freq_count)
    return (np.abs(order[:, None] - order[None, :]) <= reach).astype(np.float32).astype(BF16)


def lag_table(length, lag_count, factor):
    bins = bin_order(length // 2)[:, None]
    lags = (np.arange(lag_count) - lag_count // 2)[None, :]
    angle = 2 * np.pi * (bins * lags % length) / length
    weight = np.where(bins == 0, 1.0, 2.0) * factor
    return split_table(np.concatenate([weight * np.cos(angle), -weight * np.sin(angle)], axis=0))


def halves(value):
    high = value.astype(BF16)
    return high, (value - high.astype(F32)).astype(BF16)


def stacked(value):
    return jnp.concatenate(halves(value), axis=0)


def dot(a, b):
    return jnp.dot(a, b, preferred_element_type=F32)


def folded(product):
    half = product.shape[0] // 2
    return product[:half] + product[half:]


def fused_kernel(
    half_width, smooth_reach, chan_count, win_count,
    src_hbm, rec_hbm, fwd_hbm, band_hbm, lag_hbm, out_ref,
    src_ref, rec, xt, recv, nrm, yy, fr, fi, mm, ww, wo, gs, cc, part, land,
    fwd, band, lag,
    rec_sem, tab_sem, sent, a_recv, g_recv, w_recv, r_recv,
):
    me = lax.axis_index("chan")
    row = lax.axis_index("win")
    windows, time, _ = rec.shape
    sets = 2 * windows
    group = xt.shape[2] // windows
    rows = sets * group
    freq = fr.shape[1]
    tiles = freq // LANES
    core, x, y = lax.rem(me, 2), lax.rem(me // 2, 2), me // 4
    upper, side = row // 2, lax.rem(row, 2)
    place = 2 * side + y
    far = (1 - upper, upper)
    column = [4 * far[s] + lax.rem(me, 4) for s in range(STAGES)]

    def flip(bit, by):
        return bit + by * (1 - 2 * bit)

    def masked(mask):
        dx, dy, z = mask >> 1 & 1, mask >> 2 & 1, mask >> 3
        chan = 4 * flip(y, dy) + 2 * flip(x, dx) + flip(core, mask & 1)
        return chan, row + z * (1 - 2 * side)

    def slot_of(chan, win):
        return lax.rem(win, 2) * chan_count + chan

    mine = slot_of(me, row)
    loads = [
        pltpu.make_async_copy(rec_hbm.at[w], rec.at[w], rec_sem.at[w]) for w in range(windows)
    ]
    tables = [
        pltpu.make_async_copy(hbm, vmem, tab_sem.at[i])
        for i, (hbm, vmem) in enumerate(
            ((fwd_hbm, fwd), (band_hbm, band), (lag_hbm, lag), (src_hbm, src_ref))
        )
    ]
    for copy in loads:
        copy.start()
    barrier = pltpu.get_barrier_semaphore()
    for mask in range(1, 2 * chan_count):
        chan, win = masked(mask)
        pl.semaphore_signal(
            barrier, inc=1, device_id={"chan": chan, "win": win}, device_id_type=MESH
        )
    for s in range(STAGES):
        for k in range(2):
            pl.semaphore_signal(
                barrier, inc=1, device_id={"chan": column[s], "win": 2 * (1 - upper) + k},
                device_id_type=MESH,
            )

    for copy in tables:
        copy.start()
    for w in range(windows):
        loads[w].wait()
        for h in range(2):
            tile = rec[w, :, h * LANES : (h + 1) * LANES].T
            for i in range(LANES // group):
                slot = i % 4 // 2 * chan_count + i % 2 * 4 + i // 4
                xt[h, slot, w * group : (w + 1) * group] = tile[i * group : (i + 1) * group]

    pl.semaphore_wait(barrier, 2 * chan_count - 1 + 2 * STAGES)

    for s in range(STAGES):
        for mask in ((14, 15, 12, 13, 10, 11, 6, 7, 8, 9, 4, 5, 2, 3, 1), (15, 14, 13, 12, 11, 10, 7, 6, 9, 8, 5, 4, 3, 2, 1))[s]:
            chan, win = masked(mask)
            pltpu.make_async_remote_copy(
                src_ref=xt.at[far[s], slot_of(chan, win)], dst_ref=recv.at[s, me, side],
                send_sem=sent.at[0], recv_sem=a_recv.at[s],
                device_id={"chan": chan, "win": win}, device_id_type=MESH,
            ).start()
        pltpu.make_async_copy(xt.at[far[s], mine], recv.at[s, me, side], a_recv.at[s]).start()
    near_row = lax.broadcasted_iota(jnp.int32, (3 * time, time), 0) - time
    near_col = lax.broadcasted_iota(jnp.int32, (3 * time, time), 1)
    near = (jnp.abs(near_row - near_col) <= half_width).astype(F32).astype(BF16)
    root = math.sqrt(0.5)

    def settle(ref, sem):
        pltpu.make_async_copy(ref, ref, sem).wait()

    def normalise(s):
        for i in range(8):
            level = jnp.zeros((rows, time), F32)
            for j in range(max(i - 1, 0), min(i + 1, 7) + 1):
                both = stacked(jnp.abs(recv[s, j].reshape(rows, time)))
                level = level + folded(dot(both, near[(j - i + 1) * time : (j - i + 2) * time]))
            level = level * (1.0 / (2 * half_width + 1))
            nrm[i] = recv[s, i].reshape(rows, time) / jnp.maximum(level, AMPLITUDE_FLOOR)

    def butterfly(block, _):
        at = pl.ds(pl.multiple_of(block * 16, 16), 16)
        low_at = pl.ds(pl.multiple_of(rows + block * 16, 16), 16)
        n = [nrm[i, at, :] for i in range(8)]
        a = [n[i] + n[i + 4] for i in range(4)]
        b = [n[i] - n[i + 4] for i in range(4)]
        even, odd = a[0] + a[2], a[1] + a[3]
        diff, total = root * (b[1] - b[3]), root * (b[1] + b[3])
        pairs = (
            (even + odd, even - odd),
            (b[0] + diff, -(b[2] + total)),
            (a[0] - a[2], a[3] - a[1]),
            (b[0] - diff, b[2] - total),
        )
        for g, pair in enumerate(pairs):
            for k, value in enumerate(pair):
                high, low = halves(value)
                yy[g, at, k * time : (k + 1) * time] = high
                yy[g, low_at, k * time : (k + 1) * time] = low
        return 0

    def transform(s):
        for block in range(rows // 16):
            butterfly(block, 0)
        if s == 0:
            tables[0].wait()
        for g in range(4):
            at = slice(g * LANES, (g + 1) * LANES)
            both = folded(dot(yy[g], fwd[0, g])) + dot(yy[g, :rows], fwd[1, g])
            real, imag = both[:, :LANES], both[:, LANES:]
            fr[:, at] = real
            fi[:, at] = imag
            mm[:, at] = stacked(jnp.sqrt(real * real + imag * imag))

    def whiten(s):
        if s == 0:
            tables[1].wait()
        for g in range(freq // 256):
            at = slice(g * 256, (g + 1) * 256)
            smoothed = folded(dot(mm[...], band[:, at])) / (2 * smooth_reach + 1) + WHITE_EPSILON
            inverse = 1.0 / smoothed
            ww[s, 0, :, at] = fr[:, at] * inverse
            ww[s, 1, :, at] = fi[:, at] * inverse

    def pick(s):
        if s == 0:
            tables[3].wait()
        owned = lax.rem(src_ref[4 * column[s] + place], group)
        for w in range(sets):
            for k in range(2):
                line = 2 * w + k
                gs[s, mine, line : line + 1, :] = ww[s, k, pl.ds(w * group + owned, 1), :]

    def offer(s, mask):
        chan, win = masked(mask)
        return pltpu.make_async_remote_copy(
            src_ref=gs.at[s, mine], dst_ref=gs.at[s, mine],
            send_sem=sent.at[1], recv_sem=g_recv.at[s, mask // 2],
            device_id={"chan": chan, "win": win}, device_id_type=MESH,
        )

    def offers(s, masks):
        for mask in masks:
            offer(s, mask).start()

    def arrive(s, masks):
        for mask in masks:
            offer(s, mask).wait_recv()

    def share(s):
        chan, win = masked(1)
        return pltpu.make_async_remote_copy(
            src_ref=ww.at[s], dst_ref=wo.at[s],
            send_sem=sent.at[2], recv_sem=w_recv.at[0],
            device_id={"chan": chan, "win": win}, device_id_type=MESH,
        )

    for s in range(STAGES):
        settle(recv.at[s], a_recv.at[s])
        if s == 1:
            offers(0, (6, 12, 10, 14))
        normalise(s)
        transform(s)
        whiten(s)
        share(s).start()
        pick(s)
        offers(s, ((1, 2, 4, 8), (8,))[s])
    tables[2].wait()

    def compute(sources, entries):
        half = len(entries) * group
        targets = sorted({target for _, target in entries})
        for t in range(tiles):
            at = slice(t * LANES, (t + 1) * LANES)
            sums = {}
            for w in range(sets):
                rows_at = slice(w * group, (w + 1) * group)
                white = {
                    (j, v): tuple((ww, wo)[j][v, k, rows_at, at] for k in range(2))
                    for j, v in targets
                }
                lines = [
                    (gs[s, slot, 2 * w : 2 * w + 1, at], gs[s, slot, 2 * w + 1 : 2 * w + 2, at])
                    for s, slot in sources
                ]
                for n, (source, target) in enumerate(entries):
                    (sr, si), (real, imag) = lines[source], white[target]
                    new = (sr * real + si * imag, sr * imag - si * real)
                    for k in range(2):
                        sums[n, k] = new[k] if w == 0 else sums[n, k] + new[k]
            for n in range(0, len(entries), 2):
                for k in range(2):
                    high, low = halves(jnp.concatenate([sums[n, k], sums[n + 1, k]], axis=0))
                    col = k * freq + t * LANES
                    cc[n * group : (n + 2) * group, col : col + LANES] = high
                    cc[half + n * group : half + (n + 2) * group, col : col + LANES] = low
        return folded(dot(cc[: 2 * half], lag[0])) + dot(cc[:half], lag[1])

    def deliver(staged, landed, j, v, owner, value):
        def send():
            staged[...] = value
            pltpu.make_async_remote_copy(
                src_ref=staged, dst_ref=landed, send_sem=sent.at[3], recv_sem=r_recv.at[0],
                device_id={"win": owner, "chan": column[v] + j * (1 - 2 * core)},
                device_id_type=MESH,
            ).start()

        if j == 1:
            send()
            return
        here = (owner == row) & (column[v] == me)

        @pl.when(here)
        def _():
            landed[...] = value

        @pl.when(jnp.logical_not(here))
        def _():
            send()

    steps = 2 * win_count - 1
    base = side * chan_count + 4 * y + 2 * x
    arrive(0, (1,))
    entries = [(k, (0, v)) for v in range(STAGES) for k in range(2)]
    result = compute([(0, base), (0, base + 1)], entries)
    for n, (k, (_, v)) in enumerate(entries):
        at = slice(n * group, (n + 1) * group)
        spot = pl.ds(pl.multiple_of(y * group, group), group)
        deliver(
            part.at[2 * steps, at], land.at[upper, place, side, k, spot], 0, v,
            2 * far[0] + x, result[at],
        )
    offers(1, (2, 4, 6))
    settle(wo, w_recv.at[0])
    arrive(0, (4,))
    entries = [(0, (j, v)) for j in range(2) for v in range(STAGES)]
    result = compute([(0, side * chan_count + 4 * (1 - y) + 2 * x + core)], entries)
    for n, (_, (j, v)) in enumerate(entries):
        at = slice(n * group, (n + 1) * group)
        spot = pl.ds(pl.multiple_of((1 - y) * group, group), group)
        deliver(
            part.at[2 * steps + 2, at], land.at[upper, place, side, core, spot], j, v,
            2 * far[0] + x, result[at],
        )

    def forward():
        arrive(1, (8,))
        for target in (2, 4, 6):
            chan, win = masked(target)
            slot = gs.at[1, slot_of(*masked(8))]
            pltpu.make_async_remote_copy(
                src_ref=slot, dst_ref=slot, send_sem=sent.at[1], recv_sem=g_recv.at[1, 4 + target // 2],
                device_id={"chan": chan, "win": win}, device_id_type=MESH,
            ).start()

    def step(q, _):
        s = (q + 1) // 4
        i = q - 3 * s
        e = flip(x, 1 - upper)
        early = (2 - i) * (1 - i) // 2 * (2 - e) + i * (2 - i) * (1 + 2 * e) + i * (i - 1) // 2 * (3 - e)
        t = (1 - s) * early + s * ((side + upper - 2 * side * upper) * (2 * lax.rem(i, 2) + flip(i // 2, flip(x, upper))) + (1 - (side + upper - 2 * side * upper)) * (2 * (i // 2) + flip(lax.rem(i, 2), flip(x, upper))))
        at_x, r = flip(x, lax.rem(t, 2)), flip(side, t // 2)
        owner = 2 * (far[0] + s * (far[1] - far[0])) + at_x
        @pl.when(q == 1)
        def _():
            forward()

        for k, masks in enumerate(((4,), (2, 6), (8, 12), (10, 14))):
            for stage in range(1 - min(k, 1), STAGES):
                @pl.when((s == stage) & (t == k))
                def _():
                    arrive(stage, masks[stage:] if k == 2 else masks)

        slots = [(s, r * chan_count + 4 * there + 2 * at_x + core) for there in range(2)]
        entries = [(n, (j, v)) for j in range(2) for v in range(STAGES) for n in range(2)]
        result = compute(slots, entries)
        for j in (1, 0):
            for v in range(STAGES):
                first = (2 * j + v) * 2 * group
                deliver(
                    part.at[2 * q + j, v * 2 * group : (v + 1) * 2 * group],
                    land.at[upper, place, r, core], j, v, owner, result[first : first + 2 * group],
                )
        return 0

    lax.fori_loop(0, steps, step, 0)

    settle(part.at[: 2 * steps + 1], r_recv.at[0])
    for g in range(4):
        for r in range(2):
            for k in range(2):
                for there in range(2):
                    at = slice(there * group, (there + 1) * group)
                    to = ((4 * k + 2 * r + there) * 4 + g) * group
                    out_ref[to : to + group, :] = land[0, g, r, k, at] + land[1, g, r, k, at]

    settle(part.at[: 2 * steps + 1], sent.at[0])
    settle(gs.at[0, : 2 * chan_count - 1], sent.at[1])
    settle(ww, sent.at[2])
    settle(part.at[: 2 * steps + 1], sent.at[3])


def fused(records, sources):
    chan_count, win_count = lax.axis_size("chan"), lax.axis_size("win")
    windows, time, channels = records.shape
    length = time * chan_count
    freq = length // 2
    group = channels // chan_count // 4
    sets = 2 * windows
    rows = sets * group
    source_count = sources.shape[0]
    lag_count = length // 4
    reach = length // 32
    half_width = min(16, time)
    owned = source_count // win_count
    factor = 1.0 / math.sqrt(windows * win_count * freq)
    fwd = forward_blocks(length, time)
    band = smooth_table(freq, reach)
    lag = lag_table(length, lag_count, factor)
    width = STAGES * group
    block = owned * 2 * width
    vmem = pl.BlockSpec(memory_space=pltpu.VMEM)
    hbm = pl.BlockSpec(memory_space=pltpu.HBM)
    dma = pltpu.SemaphoreType.DMA
    out = pl.pallas_call(
        functools.partial(fused_kernel, half_width, reach, chan_count, win_count),
        out_shape=pltpu.VMEM((block, lag_count), F32),
        in_specs=[hbm] * 5,
        out_specs=vmem,
        scratch_shapes=[
            pltpu.SMEM(sources.shape, jnp.int32),
            pltpu.VMEM(records.shape, F32),
            pltpu.VMEM((2, 2 * chan_count, windows * group, time), F32),
            pltpu.VMEM((STAGES, chan_count, 2, windows * group, time), F32),
            pltpu.VMEM((chan_count, rows, time), F32),
            pltpu.VMEM((4, 2 * rows, 2 * time), BF16),
            pltpu.VMEM((rows, freq), F32),
            pltpu.VMEM((rows, freq), F32),
            pltpu.VMEM((2 * rows, freq), BF16),
            pltpu.VMEM((STAGES, 2, rows, freq), F32),
            pltpu.VMEM((STAGES, 2, rows, freq), F32),
            pltpu.VMEM((STAGES, 2 * chan_count, 2 * sets, freq), F32),
            pltpu.VMEM((16 * group, 2 * freq), BF16),
            pltpu.VMEM((4 * win_count + 2, 4 * group, lag_count), F32),
            pltpu.VMEM((2, 4, 2, 2, 2 * group, lag_count), F32),
            pltpu.VMEM(fwd.shape, BF16),
            pltpu.VMEM(band.shape, BF16),
            pltpu.VMEM(lag.shape, BF16),
            dma((windows,)),
            dma((4,)),
            dma((4,)),
            dma((STAGES,)),
            dma((STAGES, chan_count)),
            dma((1,)),
            dma((1,)),
        ],
        compiler_params=pltpu.CompilerParams(
            collective_id=0, has_side_effects=True, vmem_limit_bytes=40_000_000
        ),
        name="interferometry",
    )(*[
        pltpu.with_memory_space_constraint(value, pltpu.HBM)
        for value in (sources, records, jnp.asarray(fwd), jnp.asarray(band), jnp.asarray(lag))
    ])
    return out.reshape(owned, 2 * width, lag_count).transpose(0, 2, 1)


def fits(records, sources):
    chan_count, win_count = lax.axis_size("chan"), lax.axis_size("win")
    windows, time, channels = records.shape
    return (
        time == LANES and chan_count == 8 and win_count == 4 and channels % LANES == 0
        and channels == 32 * chan_count and sources.shape[0] == 4 * chan_count
        and windows % 2 == 0
    )


def body(records, sources):
    return fused(records, sources) if fits(records, sources) else local(records, sources)


def solution(mesh):
    placed = (P("win", "chan", None), P())
    return jax.shard_map(
        body, mesh=mesh, in_specs=placed, out_specs=P("win", None, "chan"), check_vma=False
    )
```

```python
import functools
import math

import jax
import jax.numpy as jnp
import numpy as np
from jax import lax
from jax.experimental import pallas as pl
from jax.experimental.pallas import tpu as pltpu
from jax.sharding import PartitionSpec as P

HIGHEST = lax.Precision.HIGHEST
AMPLITUDE_FLOOR = 0.25
WHITE_EPSILON = 1e-06


def fourier_table(length):
    freq_count = length // 2
    freqs = jnp.arange(freq_count, dtype=jnp.int32)[:, None]
    sample_index = jnp.arange(length, dtype=jnp.int32)[None, :]
    angles = (freqs * sample_index % length).astype(jnp.float32) * (2.0 * math.pi / length)
    return jnp.concatenate([jnp.cos(angles), -jnp.sin(angles)], axis=0)


def band_table(freq_count, reach):
    rows_index = jnp.arange(freq_count, dtype=jnp.int32)[:, None]
    cols_index = jnp.arange(freq_count, dtype=jnp.int32)[None, :]
    return (jnp.abs(rows_index - cols_index) <= reach).astype(jnp.float32)


def inverse_table(length, lag_count, first_bin, bin_count, factor):
    freqs = first_bin + jnp.arange(bin_count, dtype=jnp.int32)
    lag_index = jnp.arange(lag_count, dtype=jnp.int32) - lag_count // 2
    angles = (lag_index[:, None] * freqs[None, :] % length).astype(jnp.float32) * (
        2.0 * math.pi / length
    )
    weights = jnp.where(freqs == 0, 1.0, 2.0).astype(jnp.float32)[None, :] * factor
    return jnp.concatenate([weights * jnp.cos(angles), -weights * jnp.sin(angles)], axis=1)


def running_level(padded, time_count, window_span):
    window_total = padded.shape[0]
    chans = padded.shape[2]
    running = jnp.concatenate(
        [jnp.zeros((window_total, 1, chans), jnp.float32), jnp.cumsum(jnp.abs(padded), axis=1)],
        axis=1,
    )
    return (running[:, window_span:] - running[:, :time_count]) / window_span


def local(records, sources):
    chan_count = lax.axis_size("chan")
    local_windows, local_time, all_channels = records.shape
    length = local_time * chan_count
    freq_count = length // 2
    chan_width = all_channels // chan_count
    half_width = min(16, local_time)
    smooth_reach = length // 32
    window_span = 2 * half_width + 1
    lag_count = length // 4
    forward = fourier_table(length)
    band_matrix = band_table(freq_count, smooth_reach)
    pieces = lax.all_to_all(records, "chan", split_axis=2, concat_axis=1, tiled=True)
    padded = jnp.pad(pieces, ((0, 0), (half_width, half_width), (0, 0)))
    amplitude = running_level(padded, length, window_span)
    whiten_pieces = pieces / jnp.maximum(amplitude, AMPLITUDE_FLOOR)
    spectrum = jnp.einsum("kt,wtc->wkc", forward, whiten_pieces, precision=HIGHEST)
    real_part = spectrum[:, :freq_count]
    imag_part = spectrum[:, freq_count:]
    magnitude = jnp.sqrt(real_part * real_part + imag_part * imag_part)
    smoothed = (
        jnp.einsum("jk,wkc->wjc", band_matrix, magnitude, precision=HIGHEST)
        / (2 * smooth_reach + 1)
        + WHITE_EPSILON
    )
    whitened = jnp.stack([real_part / smoothed, imag_part / smoothed], axis=1)
    band_data = lax.all_to_all(whitened, "win", split_axis=2, concat_axis=0, tiled=True)
    total_windows = band_data.shape[0]
    band_count = band_data.shape[2]
    source_count = sources.shape[0]
    chan_index = lax.axis_index("chan")
    channel_ids = jnp.arange(chan_width, dtype=jnp.int32)
    per_device = source_count // chan_count
    owned_local = (
        lax.dynamic_slice_in_dim(sources, chan_index * per_device, per_device)
        - chan_index * chan_width
    )
    selector = (owned_local[:, None] == channel_ids[None, :]).astype(jnp.float32)
    chosen = jnp.einsum("sc,wafc->wafs", selector, band_data, precision=HIGHEST)
    spectra = lax.all_gather(chosen, "chan", axis=3, tiled=True)
    source_real = spectra[:, 0]
    source_imag = spectra[:, 1]
    white_real = band_data[:, 0]
    white_imag = band_data[:, 1]
    cross_real = jnp.einsum(
        "wfs,wfc->fsc", source_real, white_real, precision=HIGHEST
    ) + jnp.einsum("wfs,wfc->fsc", source_imag, white_imag, precision=HIGHEST)
    cross_imag = jnp.einsum(
        "wfs,wfc->fsc", source_real, white_imag, precision=HIGHEST
    ) - jnp.einsum("wfs,wfc->fsc", source_imag, white_real, precision=HIGHEST)
    stacked = jnp.stack([cross_real, cross_imag])
    factor = 1.0 / math.sqrt(total_windows * freq_count)
    band_start = lax.axis_index("win") * band_count
    band_table_part = inverse_table(length, lag_count, band_start, band_count, factor).reshape(
        lag_count, 2, band_count
    )
    return lax.psum_scatter(
        jnp.einsum("tak,aksc->stc", band_table_part, stacked, precision=HIGHEST),
        "win",
        scatter_dimension=0,
        tiled=True,
    )


LANES = 128
STAGES = 2
BF16 = jnp.bfloat16
F32 = jnp.float32
MESH = pl.DeviceIdType.MESH


def bin_order(freq_count):
    per = freq_count // 8
    pairs = ((0, 4), (1, 7), (2, 6), (3, 5))
    return np.concatenate([8 * np.arange(per) + m for pair in pairs for m in pair])


def split_table(table):
    high = table.astype(np.float32).astype(BF16)
    low = (table - high.astype(np.float64)).astype(np.float32).astype(BF16)
    return np.stack([high, low])


def forward_blocks(length, time):
    per = length // 16
    rows = np.arange(time)[:, None]
    blocks = []
    for first, second in ((0, 4), (1, 7), (2, 6), (3, 5)):
        angle1 = 2 * np.pi * ((8 * np.arange(per) + first)[None, :] * rows % length) / length
        angle2 = 2 * np.pi * ((8 * np.arange(per) + second)[None, :] * rows % length) / length
        c1, s1, c2, s2 = np.cos(angle1), np.sin(angle1), np.cos(angle2), np.sin(angle2)
        if first == 0:
            zero = np.zeros_like(c1)
            top = np.concatenate([c1, zero, -s1, zero], axis=1)
            low = np.concatenate([zero, c2, zero, -s2], axis=1)
        else:
            top = np.concatenate([c1, c2, -s1, -s2], axis=1)
            low = np.concatenate([s1, -s2, c1, -c2], axis=1)
        blocks.append(np.concatenate([top, low], axis=0))
    return split_table(np.stack(blocks))


def smooth_table(freq_count, reach):
    order = bin_order(freq_count)
    return (np.abs(order[:, None] - order[None, :]) <= reach).astype(np.float32).astype(BF16)


def lag_table(length, lag_count, factor):
    bins = bin_order(length // 2)[:, None]
    lags = (np.arange(lag_count) - lag_count // 2)[None, :]
    angle = 2 * np.pi * (bins * lags % length) / length
    weight = np.where(bins == 0, 1.0, 2.0) * factor
    return split_table(np.concatenate([weight * np.cos(angle), -weight * np.sin(angle)], axis=0))


def halves(value):
    high = value.astype(BF16)
    return high, (value - high.astype(F32)).astype(BF16)


def stacked(value):
    return jnp.concatenate(halves(value), axis=0)


def dot(a, b):
    return jnp.dot(a, b, preferred_element_type=F32)


def folded(product):
    half = product.shape[0] // 2
    return product[:half] + product[half:]


def fused_kernel(
    half_width, smooth_reach, chan_count, win_count,
    src_hbm, rec_hbm, fwd_hbm, band_hbm, lag_hbm, out_ref,
    src_ref, rec, xt, recv, nrm, yy, fr, fi, mm, ww, wo, gs, cc, part, land,
    fwd, band, lag,
    rec_sem, tab_sem, sent, a_recv, g_recv, w_recv, r_recv,
):
    me = lax.axis_index("chan")
    row = lax.axis_index("win")
    windows, time, _ = rec.shape
    sets = 2 * windows
    group = xt.shape[2] // windows
    rows = sets * group
    freq = fr.shape[1]
    tiles = freq // LANES
    core, x, y = lax.rem(me, 2), lax.rem(me // 2, 2), me // 4
    upper, side = row // 2, lax.rem(row, 2)
    place = 2 * side + y
    far = (1 - upper, upper)
    column = [4 * far[s] + lax.rem(me, 4) for s in range(STAGES)]

    def flip(bit, by):
        return bit + by * (1 - 2 * bit)

    def masked(mask):
        dx, dy, z = mask >> 1 & 1, mask >> 2 & 1, mask >> 3
        chan = 4 * flip(y, dy) + 2 * flip(x, dx) + flip(core, mask & 1)
        return chan, row + z * (1 - 2 * side)

    def slot_of(chan, win):
        return lax.rem(win, 2) * chan_count + chan

    mine = slot_of(me, row)
    loads = [
        pltpu.make_async_copy(rec_hbm.at[w], rec.at[w], rec_sem.at[w]) for w in range(windows)
    ]
    tables = [
        pltpu.make_async_copy(hbm, vmem, tab_sem.at[i])
        for i, (hbm, vmem) in enumerate(
            ((fwd_hbm, fwd), (band_hbm, band), (lag_hbm, lag), (src_hbm, src_ref))
        )
    ]
    for copy in loads:
        copy.start()
    barrier = pltpu.get_barrier_semaphore()
    for mask in range(1, 2 * chan_count):
        chan, win = masked(mask)
        pl.semaphore_signal(
            barrier, inc=1, device_id={"chan": chan, "win": win}, device_id_type=MESH
        )
    for s in range(STAGES):
        for k in range(2):
            pl.semaphore_signal(
                barrier, inc=1, device_id={"chan": column[s], "win": 2 * (1 - upper) + k},
                device_id_type=MESH,
            )

    for copy in tables:
        copy.start()
    for w in range(windows):
        loads[w].wait()
        for h in range(2):
            tile = rec[w, :, h * LANES : (h + 1) * LANES].T
            for i in range(LANES // group):
                slot = i % 4 // 2 * chan_count + i % 2 * 4 + i // 4
                xt[h, slot, w * group : (w + 1) * group] = tile[i * group : (i + 1) * group]

    pl.semaphore_wait(barrier, 2 * chan_count - 1 + 2 * STAGES)

    for s in range(STAGES):
        for mask in ((14, 15, 12, 13, 10, 11, 6, 7, 8, 9, 4, 5, 2, 3, 1), (15, 14, 13, 12, 11, 10, 9, 8, 7, 6, 5, 4, 3, 2, 1))[s]:
            chan, win = masked(mask)
            pltpu.make_async_remote_copy(
                src_ref=xt.at[far[s], slot_of(chan, win)], dst_ref=recv.at[s, me, side],
                send_sem=sent.at[0], recv_sem=a_recv.at[s],
                device_id={"chan": chan, "win": win}, device_id_type=MESH,
            ).start()
        pltpu.make_async_copy(xt.at[far[s], mine], recv.at[s, me, side], a_recv.at[s]).start()
    near_row = lax.broadcasted_iota(jnp.int32, (3 * time, time), 0) - time
    near_col = lax.broadcasted_iota(jnp.int32, (3 * time, time), 1)
    near = (jnp.abs(near_row - near_col) <= half_width).astype(F32).astype(BF16)
    root = math.sqrt(0.5)

    def settle(ref, sem):
        pltpu.make_async_copy(ref, ref, sem).wait()

    def normalise(s):
        for i in range(8):
            level = jnp.zeros((rows, time), F32)
            for j in range(max(i - 1, 0), min(i + 1, 7) + 1):
                both = stacked(jnp.abs(recv[s, j].reshape(rows, time)))
                level = level + folded(dot(both, near[(j - i + 1) * time : (j - i + 2) * time]))
            level = level * (1.0 / (2 * half_width + 1))
            nrm[i] = recv[s, i].reshape(rows, time) / jnp.maximum(level, AMPLITUDE_FLOOR)

    def butterfly(block, _):
        at = pl.ds(pl.multiple_of(block * 16, 16), 16)
        low_at = pl.ds(pl.multiple_of(rows + block * 16, 16), 16)
        n = [nrm[i, at, :] for i in range(8)]
        a = [n[i] + n[i + 4] for i in range(4)]
        b = [n[i] - n[i + 4] for i in range(4)]
        even, odd = a[0] + a[2], a[1] + a[3]
        diff, total = root * (b[1] - b[3]), root * (b[1] + b[3])
        pairs = (
            (even + odd, even - odd),
            (b[0] + diff, -(b[2] + total)),
            (a[0] - a[2], a[3] - a[1]),
            (b[0] - diff, b[2] - total),
        )
        for g, pair in enumerate(pairs):
            for k, value in enumerate(pair):
                high, low = halves(value)
                yy[g, at, k * time : (k + 1) * time] = high
                yy[g, low_at, k * time : (k + 1) * time] = low
        return 0

    def transform(s):
        for block in range(rows // 16):
            butterfly(block, 0)
        if s == 0:
            tables[0].wait()
        for g in range(4):
            at = slice(g * LANES, (g + 1) * LANES)
            both = folded(dot(yy[g], fwd[0, g])) + dot(yy[g, :rows], fwd[1, g])
            real, imag = both[:, :LANES], both[:, LANES:]
            fr[:, at] = real
            fi[:, at] = imag
            mm[:, at] = stacked(jnp.sqrt(real * real + imag * imag))

    def whiten(s):
        if s == 0:
            tables[1].wait()
        for g in range(freq // 256):
            at = slice(g * 256, (g + 1) * 256)
            smoothed = folded(dot(mm[...], band[:, at])) / (2 * smooth_reach + 1) + WHITE_EPSILON
            inverse = 1.0 / smoothed
            ww[s, 0, :, at] = fr[:, at] * inverse
            ww[s, 1, :, at] = fi[:, at] * inverse

    def pick(s):
        if s == 0:
            tables[3].wait()
        owned = lax.rem(src_ref[4 * column[s] + place], group)
        for w in range(sets):
            for k in range(2):
                line = 2 * w + k
                gs[s, mine, line : line + 1, :] = ww[s, k, pl.ds(w * group + owned, 1), :]

    def offer(s, mask):
        chan, win = masked(mask)
        return pltpu.make_async_remote_copy(
            src_ref=gs.at[s, mine], dst_ref=gs.at[s, mine],
            send_sem=sent.at[1], recv_sem=g_recv.at[s, mask // 2],
            device_id={"chan": chan, "win": win}, device_id_type=MESH,
        )

    def offers(s, masks):
        for mask in masks:
            offer(s, mask).start()

    def arrive(s, masks):
        for mask in masks:
            offer(s, mask).wait_recv()

    def share(s):
        chan, win = masked(1)
        return pltpu.make_async_remote_copy(
            src_ref=ww.at[s], dst_ref=wo.at[s],
            send_sem=sent.at[2], recv_sem=w_recv.at[0],
            device_id={"chan": chan, "win": win}, device_id_type=MESH,
        )

    for s in range(STAGES):
        settle(recv.at[s], a_recv.at[s])
        if s == 1:
            offers(0, (6, 12, 10, 14))
        normalise(s)
        transform(s)
        whiten(s)
        share(s).start()
        pick(s)
        offers(s, ((1, 2, 4, 8), (8,))[s])
    tables[2].wait()

    def compute(sources, entries):
        half = len(entries) * group
        targets = sorted({target for _, target in entries})
        for t in range(tiles):
            at = slice(t * LANES, (t + 1) * LANES)
            sums = {}
            for w in range(sets):
                rows_at = slice(w * group, (w + 1) * group)
                white = {
                    (j, v): tuple((ww, wo)[j][v, k, rows_at, at] for k in range(2))
                    for j, v in targets
                }
                lines = [
                    (gs[s, slot, 2 * w : 2 * w + 1, at], gs[s, slot, 2 * w + 1 : 2 * w + 2, at])
                    for s, slot in sources
                ]
                for n, (source, target) in enumerate(entries):
                    (sr, si), (real, imag) = lines[source], white[target]
                    new = (sr * real + si * imag, sr * imag - si * real)
                    for k in range(2):
                        sums[n, k] = new[k] if w == 0 else sums[n, k] + new[k]
            for n in range(0, len(entries), 2):
                for k in range(2):
                    high, low = halves(jnp.concatenate([sums[n, k], sums[n + 1, k]], axis=0))
                    col = k * freq + t * LANES
                    cc[n * group : (n + 2) * group, col : col + LANES] = high
                    cc[half + n * group : half + (n + 2) * group, col : col + LANES] = low
        return folded(dot(cc[: 2 * half], lag[0])) + dot(cc[:half], lag[1])

    def deliver(staged, landed, j, v, owner, value):
        def send():
            staged[...] = value
            pltpu.make_async_remote_copy(
                src_ref=staged, dst_ref=landed, send_sem=sent.at[3], recv_sem=r_recv.at[0],
                device_id={"win": owner, "chan": column[v] + j * (1 - 2 * core)},
                device_id_type=MESH,
            ).start()

        if j == 1:
            send()
            return
        here = (owner == row) & (column[v] == me)

        @pl.when(here)
        def _():
            landed[...] = value

        @pl.when(jnp.logical_not(here))
        def _():
            send()

    steps = 2 * win_count - 1
    base = side * chan_count + 4 * y + 2 * x
    arrive(0, (1,))
    entries = [(k, (0, v)) for v in range(STAGES) for k in range(2)]
    result = compute([(0, base), (0, base + 1)], entries)
    for n, (k, (_, v)) in enumerate(entries):
        at = slice(n * group, (n + 1) * group)
        spot = pl.ds(pl.multiple_of(y * group, group), group)
        deliver(
            part.at[2 * steps, at], land.at[upper, place, side, k, spot], 0, v,
            2 * far[0] + x, result[at],
        )
    offers(1, (2, 4, 6))
    settle(wo, w_recv.at[0])
    arrive(0, (4,))
    entries = [(0, (j, v)) for j in range(2) for v in range(STAGES)]
    result = compute([(0, side * chan_count + 4 * (1 - y) + 2 * x + core)], entries)
    for n, (_, (j, v)) in enumerate(entries):
        at = slice(n * group, (n + 1) * group)
        spot = pl.ds(pl.multiple_of((1 - y) * group, group), group)
        deliver(
            part.at[2 * steps + 2, at], land.at[upper, place, side, core, spot], j, v,
            2 * far[0] + x, result[at],
        )

    def forward():
        arrive(1, (8,))
        for target in (2, 4, 6):
            chan, win = masked(target)
            slot = gs.at[1, slot_of(*masked(8))]
            pltpu.make_async_remote_copy(
                src_ref=slot, dst_ref=slot, send_sem=sent.at[1], recv_sem=g_recv.at[1, 4 + target // 2],
                device_id={"chan": chan, "win": win}, device_id_type=MESH,
            ).start()

    def step(q, _):
        s = (q + 1) // 4
        i = q - 3 * s
        e = flip(x, 1 - upper)
        early = (2 - i) * (1 - i) // 2 * (2 - e) + i * (2 - i) * (1 + 2 * e) + i * (i - 1) // 2 * (3 - e)
        t = (1 - s) * early + s * ((side + upper - 2 * side * upper) * (2 * lax.rem(i, 2) + flip(i // 2, flip(x, upper))) + (1 - (side + upper - 2 * side * upper)) * (2 * (i // 2) + flip(lax.rem(i, 2), flip(x, upper))))
        at_x, r = flip(x, lax.rem(t, 2)), flip(side, t // 2)
        owner = 2 * (far[0] + s * (far[1] - far[0])) + at_x
        @pl.when(q == 1)
        def _():
            forward()

        for k, masks in enumerate(((4,), (2, 6), (8, 12), (10, 14))):
            for stage in range(1 - min(k, 1), STAGES):
                @pl.when((s == stage) & (t == k))
                def _():
                    arrive(stage, masks[stage:] if k == 2 else masks)

        slots = [(s, r * chan_count + 4 * there + 2 * at_x + core) for there in range(2)]
        entries = [(n, (j, v)) for j in range(2) for v in range(STAGES) for n in range(2)]
        result = compute(slots, entries)
        for j in (1, 0):
            for v in range(STAGES):
                first = (2 * j + v) * 2 * group
                deliver(
                    part.at[2 * q + j, v * 2 * group : (v + 1) * 2 * group],
                    land.at[upper, place, r, core], j, v, owner, result[first : first + 2 * group],
                )
        return 0

    lax.fori_loop(0, steps, step, 0)

    settle(part.at[: 2 * steps + 1], r_recv.at[0])
    for g in range(4):
        for r in range(2):
            for k in range(2):
                for there in range(2):
                    at = slice(there * group, (there + 1) * group)
                    to = ((4 * k + 2 * r + there) * 4 + g) * group
                    out_ref[to : to + group, :] = land[0, g, r, k, at] + land[1, g, r, k, at]

    settle(part.at[: 2 * steps + 1], sent.at[0])
    settle(gs.at[0, : 2 * chan_count - 1], sent.at[1])
    settle(ww, sent.at[2])
    settle(part.at[: 2 * steps + 1], sent.at[3])


def fused(records, sources):
    chan_count, win_count = lax.axis_size("chan"), lax.axis_size("win")
    windows, time, channels = records.shape
    length = time * chan_count
    freq = length // 2
    group = channels // chan_count // 4
    sets = 2 * windows
    rows = sets * group
    source_count = sources.shape[0]
    lag_count = length // 4
    reach = length // 32
    half_width = min(16, time)
    owned = source_count // win_count
    factor = 1.0 / math.sqrt(windows * win_count * freq)
    fwd = forward_blocks(length, time)
    band = smooth_table(freq, reach)
    lag = lag_table(length, lag_count, factor)
    width = STAGES * group
    block = owned * 2 * width
    vmem = pl.BlockSpec(memory_space=pltpu.VMEM)
    hbm = pl.BlockSpec(memory_space=pltpu.HBM)
    dma = pltpu.SemaphoreType.DMA
    out = pl.pallas_call(
        functools.partial(fused_kernel, half_width, reach, chan_count, win_count),
        out_shape=pltpu.VMEM((block, lag_count), F32),
        in_specs=[hbm] * 5,
        out_specs=vmem,
        scratch_shapes=[
            pltpu.SMEM(sources.shape, jnp.int32),
            pltpu.VMEM(records.shape, F32),
            pltpu.VMEM((2, 2 * chan_count, windows * group, time), F32),
            pltpu.VMEM((STAGES, chan_count, 2, windows * group, time), F32),
            pltpu.VMEM((chan_count, rows, time), F32),
            pltpu.VMEM((4, 2 * rows, 2 * time), BF16),
            pltpu.VMEM((rows, freq), F32),
            pltpu.VMEM((rows, freq), F32),
            pltpu.VMEM((2 * rows, freq), BF16),
            pltpu.VMEM((STAGES, 2, rows, freq), F32),
            pltpu.VMEM((STAGES, 2, rows, freq), F32),
            pltpu.VMEM((STAGES, 2 * chan_count, 2 * sets, freq), F32),
            pltpu.VMEM((16 * group, 2 * freq), BF16),
            pltpu.VMEM((4 * win_count + 2, 4 * group, lag_count), F32),
            pltpu.VMEM((2, 4, 2, 2, 2 * group, lag_count), F32),
            pltpu.VMEM(fwd.shape, BF16),
            pltpu.VMEM(band.shape, BF16),
            pltpu.VMEM(lag.shape, BF16),
            dma((windows,)),
            dma((4,)),
            dma((4,)),
            dma((STAGES,)),
            dma((STAGES, chan_count)),
            dma((1,)),
            dma((1,)),
        ],
        compiler_params=pltpu.CompilerParams(
            collective_id=0, has_side_effects=True, vmem_limit_bytes=40_000_000
        ),
        name="interferometry",
    )(*[
        pltpu.with_memory_space_constraint(value, pltpu.HBM)
        for value in (sources, records, jnp.asarray(fwd), jnp.asarray(band), jnp.asarray(lag))
    ])
    return out.reshape(owned, 2 * width, lag_count).transpose(0, 2, 1)


def fits(records, sources):
    chan_count, win_count = lax.axis_size("chan"), lax.axis_size("win")
    windows, time, channels = records.shape
    return (
        time == LANES and chan_count == 8 and win_count == 4 and channels % LANES == 0
        and channels == 32 * chan_count and sources.shape[0] == 4 * chan_count
        and windows % 2 == 0
    )


def body(records, sources):
    return fused(records, sources) if fits(records, sources) else local(records, sources)


def solution(mesh):
    placed = (P("win", "chan", None), P())
    return jax.shard_map(
        body, mesh=mesh, in_specs=placed, out_specs=P("win", None, "chan"), check_vma=False
    )
```
